32 devices in a mesh: gx: 8 (over z, core), gy: 4 (over y, x).
Axes of the slice: x: 2, y: 2, z: 4, core: 2. Of those that a mesh axis runs over, the one named last changes fastest.
Arguments:
- raw_stack: float32 [2, 32, 128, 2048], P(None, ('gx', 'gy')), may hold values from 0 to 8
- psf_taps: float32 [3, 2, 31], replicated, may hold values from 0.05 to 1
Outputs:
- estimate: float32 [2, 32, 128, 2048], P(None, None, 'gy', 'gx')
The draws below stay inside these ranges and needn't reach their ends.
All inputs are finite; a program needn't handle non-finite values.
Results may differ from the reference program's by a relative error of at most 0.0001.
Values sent between devices are 32-bit elements; how exact they have to be, the bound alone decides.
A program may use at most 192 MiB of HBM per device.

```python
import math
import jax
import jax.numpy as jnp
from jax import lax

CH = 2
NY = 2048
TAPS = 31
ITERS = 2
NX = 128
Z = 32


def draw_raw_stack(key, part):
    key_level = jax.random.fold_in(key, 11)
    key_stripe = jax.random.fold_in(key, 12)
    base_level = jax.random.uniform(key_level, (CH, Z, NX, NY), jnp.float32, 0.25, 4.0)
    stripe_gain = jnp.exp(jax.random.uniform(key_stripe, (CH, Z, 1, NY), jnp.float32, math.log(0.5), math.log(2.0)))
    return base_level * stripe_gain


def setup_inputs(seed: int = 0) -> dict:
    keys = jax.random.split(jax.random.key(seed), 3)
    return {
        "raw_stack": draw_raw_stack(jax.random.fold_in(keys[2], 71), 0),
        "psf_taps": jnp.clip(jnp.exp(jax.random.uniform(keys[1], (3, CH, TAPS), jnp.float32, math.log(0.05), math.log(1.0))), 0.05, 1.0),
    }


BACKGROUND = 0.5
SIGMA_ACROSS = 48.0
SIGMA_ALONG = 96.0


def smoothing_table(length_cells, spread_cells, circular):
    places = lax.iota(jnp.int32, length_cells)
    offset = jnp.abs(places[:, None] - places[None, :])
    if circular:
        offset = jnp.minimum(offset, length_cells - offset)
    scaled = offset.astype(jnp.float32) / spread_cells
    kernel_table = jnp.exp(-0.5 * scaled * scaled)
    return kernel_table / jnp.sum(kernel_table, axis=1, keepdims=True)


def filter_axis(volume, kernel_taps, axis_index):
    half_taps = kernel_taps.shape[1] // 2
    results = []
    for channel in range(volume.shape[0]):
        shifted_axes = jnp.moveaxis(volume[channel], axis_index - 1, -1)
        line_rows = shifted_axes.reshape(-1, 1, shifted_axes.shape[-1])
        kernel = kernel_taps[channel].reshape(1, 1, -1)
        output = lax.conv_general_dilated(line_rows, kernel, (1,), [(half_taps, half_taps)], precision=lax.Precision.HIGHEST)
        results.append(jnp.moveaxis(output.reshape(shifted_axes.shape), -1, axis_index - 1))
    return jnp.stack(results)


def blur_volume(volume, kernel_set):
    result = filter_axis(volume, kernel_set[0], 1)
    result = filter_axis(result, kernel_set[1], 2)
    return filter_axis(result, kernel_set[2], 3)


def reference(raw_stack, psf_taps):
    across_table = smoothing_table(NX, SIGMA_ACROSS, False)
    along_table = smoothing_table(NY, SIGMA_ALONG, True)

    def destripe(plane):
        smoothed = jnp.einsum('ij,cjy->ciy', across_table, plane, precision=lax.Precision.HIGHEST)
        stripes = smoothed - jnp.einsum('cxj,jy->cxy', smoothed, along_table, precision=lax.Precision.HIGHEST)
        return jnp.maximum(plane - stripes, 0.0)

    cleaned = jnp.moveaxis(lax.map(destripe, jnp.moveaxis(raw_stack, 1, 0)), 0, 1)
    forward = psf_taps / jnp.sum(psf_taps, axis=2, keepdims=True)
    backward = forward[:, :, ::-1]
    estimate = cleaned
    for iteration in range(ITERS):
        blurred = blur_volume(estimate, forward)
        ratio_field = cleaned / (blurred + BACKGROUND)
        estimate = estimate * blur_volume(ratio_field, backward)
    return estimate
```

```python
import functools

import jax
import jax.numpy as jnp
from jax import lax
from jax.experimental import pallas as pl
from jax.experimental.pallas import tpu as pltpu
from jax.sharding import PartitionSpec as P

ITERS = 2
BACKGROUND = 0.5
SIGMA_ACROSS = 48.0
SIGMA_ALONG = 96.0
SUB = 8
CHUNKS = 4
MESH = pl.DeviceIdType.MESH


def smoothing_table(length_cells, spread_cells):
    rows = lax.broadcasted_iota(jnp.int32, (length_cells, length_cells), 0)
    columns = lax.broadcasted_iota(jnp.int32, (length_cells, length_cells), 1)
    scaled = (rows - columns).astype(jnp.float32) / spread_cells
    kernel_table = jnp.exp(-0.5 * scaled * scaled)
    return kernel_table / jnp.sum(kernel_table, axis=1, keepdims=True)


def circular_row(length_cells, spread_cells):
    places = lax.broadcasted_iota(jnp.int32, (1, length_cells), 1)
    scaled = jnp.minimum(places, length_cells - places).astype(jnp.float32) / spread_cells
    kernel_row = jnp.exp(-0.5 * scaled * scaled)
    return kernel_row / jnp.sum(kernel_row, axis=1, keepdims=True)


def base_rows(taps, axis, channel, reach, lag_of):
    count = taps.shape[2]
    width = -(-2 * reach // 128) * 128
    place = lax.broadcasted_iota(jnp.int32, (1, width), 1)
    lag = lag_of(jnp.where(place < width // 2, place, place - width))
    forward = jnp.zeros((1, width), jnp.float32)
    backward = forward
    total = forward
    for k in range(count):
        tap = taps[axis, channel, k]
        total = total + tap
        forward = jnp.where(lag == k, tap, forward)
        backward = jnp.where(lag == count - 1 - k, tap, backward)
    return forward / total, backward / total


def shifted(base, start, count, columns):
    block = jnp.broadcast_to(base, (count, base.shape[1]))
    block = pltpu.roll(block, start, 1, stride=1, stride_axis=0)[:, :columns]
    high = block.astype(jnp.bfloat16)
    return high, (block - high.astype(jnp.float32)).astype(jnp.bfloat16)


def fill_tables(taps, channel, edge, cells, depth, rows, middle, ends):
    planes, width = depth.shape[1], rows.shape[1] // 2
    half = taps.shape[2] // 2
    depth_base = base_rows(taps, 0, channel, planes, lambda d: d + half)
    rows_base = base_rows(taps, 1, channel, width, lambda d: half - d)
    lines_base = base_rows(taps, 2, channel, max(cells, 3 * edge), lambda d: d - edge + half)
    for way in range(2):
        high, low = shifted(depth_base[way], 0, planes, planes)
        depth[way] = jnp.concatenate([high, high, low], axis=1)
        high, low = shifted(rows_base[way], 0, width, width)
        both = jnp.concatenate([high, low], axis=1)
        rows[way] = jnp.concatenate([both, both], axis=0)
        if cells > 2 * edge:
            high, low = shifted(lines_base[way], 0, cells - 2 * edge, cells)
            middle[way] = twice(high, low)
        high, low = shifted(lines_base[way], 0, edge, 3 * edge)
        ends[way] = twice(high, low)


def twice(high, low):
    both = jnp.concatenate([high, low], axis=0)
    return jnp.concatenate([both, both], axis=1)


def halves(value):
    high = value.astype(jnp.bfloat16)
    return high, (value - high.astype(jnp.float32)).astype(jnp.bfloat16)


def split(value, axis):
    return jnp.concatenate(halves(value), axis=axis)


def place_of(count_gy, pair, gy):
    first = gy // 2
    along = 2 * first + (gy % 2 + first) % 2
    odd = pair % 2
    return (1 - odd) * along + odd * (count_gy - 1 - along)


def device_of(count_gy, line):
    pair, place = line // count_gy, line % count_gy
    odd = pair % 2
    along = (1 - odd) * place + odd * (count_gy - 1 - place)
    first = along // 2
    return pair, 2 * first + (along % 2 + first) % 2


def deconvolve_kernel(
    count_gx, count_gy, edge, raw, taps, out,
    cleaned, estimate, ratio, wide0, wide1, leaving, stage, along, smooth, across, depth, rows, middle, ends,
    held, send_sem, recv_sem, out_send, out_recv, own_sem, plane_send, plane_recv, held_sem,
):
    groups, planes, _, width = cleaned.shape
    cells = groups * SUB
    size = planes * SUB
    wide = (wide0, wide1)
    gx, gy = lax.axis_index("gx"), lax.axis_index("gy")
    pair, core = gx // 2, gx % 2
    place = place_of(count_gy, pair, gy)
    line = pair * count_gy + place
    last = count_gx // 2 * count_gy - 1
    per_gx = count_gy // 2
    lines_x = width // count_gy
    me = gx * count_gy + gy

    def load(channel):
        return pltpu.make_async_copy(raw.at[channel, 0], held, held_sem)

    load(0).start()
    barrier = pltpu.get_barrier_semaphore()

    @pl.loop(0, count_gx * count_gy)
    def _(other):
        @pl.when(other != me)
        def _():
            pl.semaphore_signal(
                barrier, inc=1, device_id=(other // count_gy, other % count_gy), device_id_type=MESH
            )

    channels, _, _, lines_y = raw.shape
    block = along.shape[0] // 2
    blocks = lines_y // block
    chunks = lines_y // cells
    per_block = block // cells
    table = smoothing_table(width, SIGMA_ACROSS)
    high = table.astype(jnp.bfloat16)
    across[0:width] = high
    across[width : 2 * width] = (table - high.astype(jnp.float32)).astype(jnp.bfloat16)
    high, low = shifted(circular_row(lines_y, SIGMA_ALONG), 0, block, lines_y)
    along[0:block] = high
    along[block : 2 * block] = low

    def smooth_block(index):
        columns = pl.ds(pl.multiple_of(index * block, block), block)
        value = held[:, columns]
        high = value.astype(jnp.bfloat16)
        low = (value - high.astype(jnp.float32)).astype(jnp.bfloat16)
        product = jnp.dot(across[...], high, preferred_element_type=jnp.float32)
        total = product[:width] + product[width:]
        total += jnp.dot(across[0:width], low, preferred_element_type=jnp.float32)
        high = total.astype(jnp.bfloat16)
        smooth[0:width, columns] = high
        smooth[width : 2 * width, columns] = (total - high.astype(jnp.float32)).astype(jnp.bfloat16)

    def clean_block(channel, index):
        total = jnp.zeros((width, block), jnp.float32)
        for other in range(blocks):
            columns = pl.ds(other * block, block)
            shift = lax.rem(index - other + blocks, blocks)
            table = pl.ds(pl.multiple_of(shift * block, block), block)
            product = jnp.dot(
                smooth[:, columns], along[0:block, table], preferred_element_type=jnp.float32
            )
            total += product[:width] + product[width:]
            total += jnp.dot(
                smooth[0:width, columns], along[block : 2 * block, table],
                preferred_element_type=jnp.float32,
            )
        columns = pl.ds(pl.multiple_of(index * block, block), block)
        smoothed = smooth[0:width, columns].astype(jnp.float32)
        smoothed += smooth[width : 2 * width, columns].astype(jnp.float32)
        value = jnp.maximum(held[:, columns] - (smoothed - total), 0.0)
        leaving[pl.ds(channel * chunks + index * per_block, per_block)] = value.T.reshape(
            per_block, groups, SUB, width
        )

    def plane_copy(channel, chunk):
        target_pair, target_gy = device_of(count_gy, chunk)
        return pltpu.make_async_remote_copy(
            src_ref=leaving.at[channel * chunks + chunk],
            dst_ref=cleaned.at[:, me],
            send_sem=plane_send.at[channel * chunks + chunk],
            recv_sem=plane_recv.at[me],
            device_id=(target_pair * 2 + channel, target_gy),
            device_id_type=MESH,
        )

    own_plane = pltpu.make_async_copy(
        leaving.at[core * chunks + line], cleaned.at[:, me], plane_send.at[core * chunks + line]
    )

    def is_own_plane(channel, chunk):
        return jnp.logical_and(channel == core, chunk == line)

    for channel in range(channels):
        if channel > 0:
            load(channel).start()
        load(channel).wait()

        @pl.loop(0, blocks, unroll=2)
        def _(index):
            smooth_block(index)

        if channel == 0:
            pl.semaphore_wait(barrier, count_gx * count_gy - 1)

        @pl.loop(0, blocks)
        def _(step):
            index = lax.rem(step + (line + 1) // per_block + blocks // 2, blocks)
            clean_block(channel, index)
            for part in range(per_block):
                chunk = index * per_block + part

                @pl.when(is_own_plane(channel, chunk))
                def _():
                    own_plane.start()

                @pl.when(jnp.logical_not(is_own_plane(channel, chunk)))
                def _():
                    plane_copy(channel, chunk).start()

    fill_tables(taps, core, edge, cells, depth, rows, middle, ends)

    outer = edge // SUB
    zeros = jnp.zeros((outer, planes, SUB, width), jnp.float32)

    @pl.when(line == 0)
    def _():
        for slot in range(2):
            wide[slot][0:outer] = zeros

    @pl.when(line == last)
    def _():
        for slot in range(2):
            wide[slot][outer + groups :] = zeros

    own_plane.wait()
    for channel in range(channels):

        @pl.loop(0, chunks)
        def _(chunk):
            @pl.when(jnp.logical_not(is_own_plane(channel, chunk)))
            def _():
                plane_copy(channel, chunk).wait_send()

    @pl.loop(0, count_gx * count_gy)
    def _(other):
        @pl.when(other != me)
        def _():
            pltpu.make_async_remote_copy(
                src_ref=leaving.at[0],
                dst_ref=cleaned.at[:, other],
                send_sem=plane_send.at[0],
                recv_sem=plane_recv.at[other],
                device_id=(gx, gy),
                device_id_type=MESH,
            ).wait_recv()

    def edge_copy(slot, up):
        target_pair, target_gy = device_of(count_gy, line + (1 if up else -1))
        source = groups if up else outer
        target = 0 if up else outer + groups
        side = 1 if up else 0
        return pltpu.make_async_remote_copy(
            src_ref=wide[slot].at[pl.ds(source, outer)],
            dst_ref=wide[slot].at[pl.ds(target, outer)],
            send_sem=send_sem.at[slot, side],
            recv_sem=recv_sem.at[slot, side],
            device_id=(target_pair * 2 + core, target_gy),
            device_id_type=MESH,
        )

    def get_cell(ref, group, cell):
        if width > 128:
            return ref[group, :, cell, :]
        start = pl.multiple_of(group * size, size)
        return ref.reshape(ref.shape[0] * size, width)[pl.ds(start + cell, planes, stride=SUB), :]

    def set_cell(ref, group, cell, value):
        if width > 128:
            ref[group, :, cell, :] = value
        else:
            start = pl.multiple_of(group * size, size)
            ref.reshape(ref.shape[0] * size, width)[pl.ds(start + cell, planes, stride=SUB), :] = value

    def planes_and_rows(field, slot, way, places):
        pieces = []
        for group in places:
            for cell in range(0, SUB, 2):
                value = [get_cell(field, group, cell + k) for k in range(2)]
                high, low = halves(jnp.concatenate(value, axis=1))
                value = jnp.concatenate([high, low, high], axis=0)
                value = jnp.dot(depth[way], value, preferred_element_type=jnp.float32)
                pieces += [value[:, :width], value[:, width:]]
        value = split(jnp.concatenate(pieces, axis=0), 1)
        value = jnp.dot(value, rows[way], preferred_element_type=jnp.float32)
        value = value[:, :width] + value[:, width:]
        for at, group in enumerate(places):
            for cell in range(SUB):
                first = (at * SUB + cell) * planes
                set_cell(wide[slot], outer + group, cell, value[first : first + planes])

    inner = cells - 2 * edge

    def lines(ref, plane, first, count):
        return ref[pl.ds(first, count), plane].reshape(count * SUB, width)

    def keep(ref, plane, first, value):
        count = value.shape[0] // SUB
        ref[pl.ds(first, count), plane] = value.reshape(count, SUB, width)

    def along_table(table, count, value):
        value = jnp.dot(table, split(value, 0), preferred_element_type=jnp.float32)
        value = value[:count] + value[count:]
        return value[:, :width], value[:, width:]

    def along_middle(slot, way, plane):
        value = [lines(wide[slot], plane + k, outer, groups) for k in range(2)]
        return along_table(middle[way], inner, jnp.concatenate(value, axis=1))

    def along_ends(slot, way, plane):
        low = lines(wide[slot], plane, 0, 3 * outer)
        high = lines(wide[slot], plane, groups - outer, 3 * outer)
        return along_table(ends[way], edge, jnp.concatenate([low, high], axis=1))

    small = size * width <= 65536
    unroll = 8 if small else 1
    batch = 4 if small else 1

    def filter_places(field, slot, way, places):
        for first in range(0, len(places), batch):
            planes_and_rows(field, slot, way, places[first : first + batch])

    def filter_ends(field, slot, way):
        filter_places(field, slot, way, [*range(outer), *range(groups - outer, groups)])

        @pl.when(line > 0)
        def _():
            edge_copy(slot, False).start()

        @pl.when(line < last)
        def _():
            edge_copy(slot, True).start()

    def filter_middle(field, slot, way):
        count = groups - 2 * outer
        step = batch if count % batch == 0 else 1
        if inner:

            @pl.loop(0, count // step)
            def _(turn):
                first = outer + turn * step
                planes_and_rows(field, slot, way, [first + k for k in range(step)])

    def wait_ends(slot):
        @pl.when(line > 0)
        def _():
            edge_copy(slot, False).wait_send()
            edge_copy(slot, True).wait_recv()

        @pl.when(line < last)
        def _():
            edge_copy(slot, True).wait_send()
            edge_copy(slot, False).wait_recv()

    def out_copy(chunk, target_gy):
        part = pl.ds(chunk * (planes // CHUNKS), planes // CHUNKS)
        return pltpu.make_async_remote_copy(
            src_ref=stage.at[target_gy, part],
            dst_ref=out.at[core, place % per_gx, part],
            send_sem=out_send.at[chunk, target_gy],
            recv_sem=out_recv.at[chunk, core, place % per_gx],
            device_id=(pair * 2 + place // per_gx, target_gy),
            device_id_type=MESH,
        )

    def own_copy(chunk):
        part = pl.ds(chunk * (planes // CHUNKS), planes // CHUNKS)
        return pltpu.make_async_copy(
            stage.at[gy, part], out.at[core, place % per_gx, part], own_sem.at[chunk]
        )

    def is_own(target_gy):
        return jnp.logical_and(target_gy == gy, place // per_gx == core)

    top = groups - outer

    def middle_lines(slot, way, use):
        if inner:

            @pl.loop(0, planes // 2, unroll=max(unroll // 2, 1))
            def _(turn):
                for k, value in enumerate(along_middle(slot, way, 2 * turn)):
                    use(2 * turn + k, value)

    def to_ratio(plane, first, value):
        known = lines(cleaned, plane, first, value.shape[0] // SUB)
        keep(ratio, plane, first, known / (value + BACKGROUND))

    filter_ends(cleaned, 0, 0)
    for iteration in range(ITERS):
        source = cleaned if iteration == 0 else estimate

        def to_estimate(plane, first, value):
            keep(estimate, plane, first, lines(source, plane, first, value.shape[0] // SUB) * value)

        filter_middle(source, 0, 0)
        middle_lines(0, 0, lambda plane, value: to_ratio(plane, outer, value))
        wait_ends(0)

        @pl.loop(0, planes, unroll=unroll)
        def _(plane):
            low, high = along_ends(0, 0, plane)
            to_ratio(plane, 0, low)
            to_ratio(plane, top, high)

        filter_ends(ratio, 1, 1)
        filter_middle(ratio, 1, 1)
        middle_lines(1, 1, lambda plane, value: to_estimate(plane, outer, value))
        wait_ends(1)
        if iteration < ITERS - 1:

            @pl.loop(0, planes, unroll=unroll)
            def _(plane):
                low, high = along_ends(1, 1, plane)
                to_estimate(plane, 0, low)
                to_estimate(plane, top, high)

            filter_ends(estimate, 0, 0)
        else:
            for chunk in range(CHUNKS):

                @pl.loop(chunk * (planes // CHUNKS), (chunk + 1) * (planes // CHUNKS), unroll=unroll)
                def _(plane):
                    low, high = along_ends(1, 1, plane)
                    pieces = [lines(source, plane, 0, outer) * low]
                    if inner:
                        pieces.append(lines(estimate, plane, outer, groups - 2 * outer))
                    pieces.append(lines(source, plane, top, outer) * high)
                    value = jnp.concatenate(pieces, axis=0).T
                    for target in range(count_gy):
                        stage[target, plane] = value[target * lines_x : (target + 1) * lines_x]

                for step in range(count_gy):
                    target = lax.rem(gy + 1 + step, count_gy)

                    @pl.when(is_own(target))
                    def _():
                        own_copy(chunk).start()

                    @pl.when(jnp.logical_not(is_own(target)))
                    def _():
                        out_copy(chunk, target).start()

    for chunk in range(CHUNKS):
        part = pl.ds(chunk * (planes // CHUNKS), planes // CHUNKS)
        for target in range(count_gy):

            @pl.when(is_own(target))
            def _():
                own_copy(chunk).wait()

            @pl.when(jnp.logical_not(is_own(target)))
            def _():
                out_copy(chunk, target).wait_send()

        for channel in range(2):
            for slot in range(per_gx):
                mine = jnp.logical_and(channel == core, place == core * per_gx + slot)

                @pl.when(jnp.logical_not(mine))
                def _():
                    pltpu.make_async_remote_copy(
                        src_ref=stage.at[0, part],
                        dst_ref=out.at[channel, slot, part],
                        send_sem=out_send.at[chunk, 0],
                        recv_sem=out_recv.at[chunk, channel, slot],
                        device_id=(gx, gy),
                        device_id_type=MESH,
                    ).wait_recv()


def local(raw_stack, psf_taps):
    channels, own_planes, lines_x, lines_y = raw_stack.shape
    half_taps = psf_taps.shape[2] // 2
    count_gx = lax.axis_size("gx")
    count_gy = lax.axis_size("gy")
    pairs = count_gx // channels
    cells = lines_y // (pairs * count_gy)
    planes = own_planes * count_gx * count_gy
    edge = -(-half_taps // SUB) * SUB

    block = min(lines_y, 256)
    groups = cells // SUB
    outer = edge // SUB
    per_gx = count_gy // 2
    block_x = lines_x // count_gy
    field = pltpu.VMEM((groups, planes, SUB, lines_x), jnp.float32)
    wide = pltpu.VMEM((groups + 2 * outer, planes, SUB, lines_x), jnp.float32)
    gathered = pl.pallas_call(
        functools.partial(deconvolve_kernel, count_gx, count_gy, edge),
        out_shape=jax.ShapeDtypeStruct((channels, per_gx, planes, block_x, cells), jnp.float32),
        in_specs=[pl.BlockSpec(memory_space=pl.ANY), pl.BlockSpec(memory_space=pltpu.SMEM)],
        out_specs=pl.BlockSpec(memory_space=pl.ANY),
        scratch_shapes=[
            field,
            field,
            field,
            wide,
            wide,
            pltpu.VMEM((planes, groups, SUB, lines_x), jnp.float32),
            pltpu.VMEM((count_gy, planes, block_x, cells), jnp.float32),
            pltpu.VMEM((2 * block, lines_y), jnp.bfloat16),
            pltpu.VMEM((2 * lines_x, lines_y), jnp.bfloat16),
            pltpu.VMEM((2 * lines_x, lines_x), jnp.bfloat16),
            pltpu.VMEM((2, planes, 3 * planes), jnp.bfloat16),
            pltpu.VMEM((2, 2 * lines_x, 2 * lines_x), jnp.bfloat16),
            pltpu.VMEM((2, 2 * max(cells - 2 * edge, edge), 2 * cells), jnp.bfloat16),
            pltpu.VMEM((2, 2 * edge, 6 * edge), jnp.bfloat16),
            pltpu.VMEM((lines_x, lines_y), jnp.float32),
            pltpu.SemaphoreType.DMA((2, 2)),
            pltpu.SemaphoreType.DMA((2, 2)),
            pltpu.SemaphoreType.DMA((CHUNKS, count_gy)),
            pltpu.SemaphoreType.DMA((CHUNKS, channels, per_gx)),
            pltpu.SemaphoreType.DMA((CHUNKS,)),
            pltpu.SemaphoreType.DMA((planes,)),
            pltpu.SemaphoreType.DMA((planes,)),
            pltpu.SemaphoreType.DMA,
        ],
        compiler_params=pltpu.CompilerParams(
            collective_id=0, has_side_effects=True, vmem_limit_bytes=67043328
        ),
    )(raw_stack, psf_taps)
    return jnp.transpose(gathered, (0, 2, 3, 1, 4)).reshape(
        channels, planes, block_x, per_gx * cells
    )


def solution(mesh):
    in_specs = (P(None, ("gx", "gy"), None, None), P())
    out_specs = P(None, None, "gy", "gx")
    return jax.shard_map(local, mesh=mesh, in_specs=in_specs, out_specs=out_specs, check_vma=False)
```

```python
import functools

import jax
import jax.numpy as jnp
from jax import lax
from jax.experimental import pallas as pl
from jax.experimental.pallas import tpu as pltpu
from jax.sharding import PartitionSpec as P

ITERS = 2
BACKGROUND = 0.5
SIGMA_ACROSS = 48.0
SIGMA_ALONG = 96.0
SUB = 8
CHUNKS = 4
MESH = pl.DeviceIdType.MESH


def smoothing_table(length_cells, spread_cells):
    rows = lax.broadcasted_iota(jnp.int32, (length_cells, length_cells), 0)
    columns = lax.broadcasted_iota(jnp.int32, (length_cells, length_cells), 1)
    scaled = (rows - columns).astype(jnp.float32) / spread_cells
    kernel_table = jnp.exp(-0.5 * scaled * scaled)
    return kernel_table / jnp.sum(kernel_table, axis=1, keepdims=True)


def circular_row(length_cells, spread_cells):
    places = lax.broadcasted_iota(jnp.int32, (1, length_cells), 1)
    scaled = jnp.minimum(places, length_cells - places).astype(jnp.float32) / spread_cells
    kernel_row = jnp.exp(-0.5 * scaled * scaled)
    return kernel_row / jnp.sum(kernel_row, axis=1, keepdims=True)


def base_rows(taps, axis, channel, reach, lag_of):
    count = taps.shape[2]
    width = -(-2 * reach // 128) * 128
    place = lax.broadcasted_iota(jnp.int32, (1, width), 1)
    lag = lag_of(jnp.where(place < width // 2, place, place - width))
    forward = jnp.zeros((1, width), jnp.float32)
    backward = forward
    total = forward
    for k in range(count):
        tap = taps[axis, channel, k]
        total = total + tap
        forward = jnp.where(lag == k, tap, forward)
        backward = jnp.where(lag == count - 1 - k, tap, backward)
    return forward / total, backward / total


def shifted(base, start, count, columns):
    block = jnp.broadcast_to(base, (count, base.shape[1]))
    block = pltpu.roll(block, start, 1, stride=1, stride_axis=0)[:, :columns]
    high = block.astype(jnp.bfloat16)
    return high, (block - high.astype(jnp.float32)).astype(jnp.bfloat16)


def fill_tables(taps, channel, edge, cells, depth, rows, middle, ends):
    planes, width = depth.shape[1], rows.shape[1] // 2
    half = taps.shape[2] // 2
    depth_base = base_rows(taps, 0, channel, planes, lambda d: d + half)
    rows_base = base_rows(taps, 1, channel, width, lambda d: half - d)
    lines_base = base_rows(taps, 2, channel, max(cells, 3 * edge), lambda d: d - edge + half)
    for way in range(2):
        high, low = shifted(depth_base[way], 0, planes, planes)
        depth[way] = jnp.concatenate([high, high, low], axis=1)
        high, low = shifted(rows_base[way], 0, width, width)
        both = jnp.concatenate([high, low], axis=1)
        rows[way] = jnp.concatenate([both, both], axis=0)
        if cells > 2 * edge:
            high, low = shifted(lines_base[way], 0, cells - 2 * edge, cells)
            middle[way] = twice(high, low)
        high, low = shifted(lines_base[way], 0, edge, 3 * edge)
        ends[way] = twice(high, low)


def twice(high, low):
    both = jnp.concatenate([high, low], axis=0)
    return jnp.concatenate([both, both], axis=1)


def halves(value):
    high = value.astype(jnp.bfloat16)
    return high, (value - high.astype(jnp.float32)).astype(jnp.bfloat16)


def split(value, axis):
    return jnp.concatenate(halves(value), axis=axis)


def turned(count_gy, pair, along):
    odd = pair % 2
    return (1 - odd) * along + odd * (count_gy - 1 - along)


def device_of(count_gy, channels, channel, line):
    pair = line // count_gy
    along = turned(count_gy, pair, line % count_gy)
    return pair * 2 + along % 2, channel * (count_gy // channels) + along // 2


def deconvolve_kernel(
    count_gx, count_gy, edge, raw, taps, out,
    cleaned, estimate, ratio, wide0, wide1, leaving, stage, along, smooth, across, depth, rows, middle, ends,
    held, send_sem, recv_sem, out_send, out_recv, own_sem, plane_send, plane_recv, held_sem,
):
    groups, planes, _, width = cleaned.shape
    cells = groups * SUB
    size = planes * SUB
    wide = (wide0, wide1)
    gx, gy = lax.axis_index("gx"), lax.axis_index("gy")
    pair, core = gx // 2, gx % 2
    channels, _, _, lines_y = raw.shape
    per_channel = count_gy // channels
    mine = gy // per_channel
    place = turned(count_gy, pair, gy % per_channel * 2 + core)
    line = pair * count_gy + place
    last = count_gx // 2 * count_gy - 1
    per_gx = count_gy // 2
    lines_x = width // count_gy
    me = gx * count_gy + gy

    def load(channel):
        return pltpu.make_async_copy(raw.at[channel, 0], held, held_sem)

    def channel_of(turn):
        return lax.rem(turn + core, channels)

    load(channel_of(0)).start()
    barrier = pltpu.get_barrier_semaphore()

    @pl.loop(0, count_gx * count_gy)
    def _(other):
        @pl.when(other != me)
        def _():
            pl.semaphore_signal(
                barrier, inc=1, device_id=(other // count_gy, other % count_gy), device_id_type=MESH
            )

    block = along.shape[0] // 2
    blocks = lines_y // block
    chunks = lines_y // cells
    per_block = block // cells
    table = smoothing_table(width, SIGMA_ACROSS)
    high = table.astype(jnp.bfloat16)
    across[0:width] = high
    across[width : 2 * width] = (table - high.astype(jnp.float32)).astype(jnp.bfloat16)
    high, low = shifted(circular_row(lines_y, SIGMA_ALONG), 0, block, lines_y)
    along[0:block] = high
    along[block : 2 * block] = low

    def smooth_block(index):
        columns = pl.ds(pl.multiple_of(index * block, block), block)
        value = held[:, columns]
        high = value.astype(jnp.bfloat16)
        low = (value - high.astype(jnp.float32)).astype(jnp.bfloat16)
        product = jnp.dot(across[...], high, preferred_element_type=jnp.float32)
        total = product[:width] + product[width:]
        total += jnp.dot(across[0:width], low, preferred_element_type=jnp.float32)
        high = total.astype(jnp.bfloat16)
        smooth[0:width, columns] = high
        smooth[width : 2 * width, columns] = (total - high.astype(jnp.float32)).astype(jnp.bfloat16)

    def clean_block(channel, index):
        total = jnp.zeros((width, block), jnp.float32)
        for other in range(blocks):
            columns = pl.ds(other * block, block)
            shift = lax.rem(index - other + blocks, blocks)
            table = pl.ds(pl.multiple_of(shift * block, block), block)
            product = jnp.dot(
                smooth[:, columns], along[0:block, table], preferred_element_type=jnp.float32
            )
            total += product[:width] + product[width:]
            total += jnp.dot(
                smooth[0:width, columns], along[block : 2 * block, table],
                preferred_element_type=jnp.float32,
            )
        columns = pl.ds(pl.multiple_of(index * block, block), block)
        smoothed = smooth[0:width, columns].astype(jnp.float32)
        smoothed += smooth[width : 2 * width, columns].astype(jnp.float32)
        value = jnp.maximum(held[:, columns] - (smoothed - total), 0.0)
        leaving[pl.ds(channel * chunks + index * per_block, per_block)] = value.T.reshape(
            per_block, groups, SUB, width
        )

    def plane_copy(channel, chunk):
        target_gx, target_gy = device_of(count_gy, channels, channel, chunk)
        return pltpu.make_async_remote_copy(
            src_ref=leaving.at[channel * chunks + chunk],
            dst_ref=cleaned.at[:, me],
            send_sem=plane_send.at[channel * chunks + chunk],
            recv_sem=plane_recv.at[me],
            device_id=(target_gx, target_gy),
            device_id_type=MESH,
        )

    own_plane = pltpu.make_async_copy(
        leaving.at[mine * chunks + line], cleaned.at[:, me], plane_send.at[mine * chunks + line]
    )

    def is_own_plane(channel, chunk):
        return jnp.logical_and(channel == mine, chunk == line)

    for turn in range(channels):
        channel = channel_of(turn)
        if turn > 0:
            load(channel).start()
        load(channel).wait()

        @pl.loop(0, blocks, unroll=2)
        def _(index):
            smooth_block(index)

        if turn == 0:
            pl.semaphore_wait(barrier, count_gx * count_gy - 1)

        @pl.loop(0, blocks)
        def _(step):
            index = lax.rem(step + (line + 1) // per_block + blocks // 2, blocks)
            clean_block(channel, index)
            for part in range(per_block):
                chunk = index * per_block + part

                @pl.when(is_own_plane(channel, chunk))
                def _():
                    own_plane.start()

                @pl.when(jnp.logical_not(is_own_plane(channel, chunk)))
                def _():
                    plane_copy(channel, chunk).start()

    fill_tables(taps, mine, edge, cells, depth, rows, middle, ends)

    outer = edge // SUB
    zeros = jnp.zeros((outer, planes, SUB, width), jnp.float32)

    @pl.when(line == 0)
    def _():
        for slot in range(2):
            wide[slot][0:outer] = zeros

    @pl.when(line == last)
    def _():
        for slot in range(2):
            wide[slot][outer + groups :] = zeros

    own_plane.wait()
    for channel in range(channels):

        @pl.loop(0, chunks)
        def _(chunk):
            @pl.when(jnp.logical_not(is_own_plane(channel, chunk)))
            def _():
                plane_copy(channel, chunk).wait_send()

    @pl.loop(0, count_gx * count_gy)
    def _(other):
        @pl.when(other != me)
        def _():
            pltpu.make_async_remote_copy(
                src_ref=leaving.at[0],
                dst_ref=cleaned.at[:, other],
                send_sem=plane_send.at[0],
                recv_sem=plane_recv.at[other],
                device_id=(gx, gy),
                device_id_type=MESH,
            ).wait_recv()

    def edge_copy(slot, up):
        target_gx, target_gy = device_of(count_gy, channels, mine, line + (1 if up else -1))
        source = groups if up else outer
        target = 0 if up else outer + groups
        side = 1 if up else 0
        return pltpu.make_async_remote_copy(
            src_ref=wide[slot].at[pl.ds(source, outer)],
            dst_ref=wide[slot].at[pl.ds(target, outer)],
            send_sem=send_sem.at[slot, side],
            recv_sem=recv_sem.at[slot, side],
            device_id=(target_gx, target_gy),
            device_id_type=MESH,
        )

    def get_cell(ref, group, cell):
        if width > 128:
            return ref[group, :, cell, :]
        start = pl.multiple_of(group * size, size)
        return ref.reshape(ref.shape[0] * size, width)[pl.ds(start + cell, planes, stride=SUB), :]

    def set_cell(ref, group, cell, value):
        if width > 128:
            ref[group, :, cell, :] = value
        else:
            start = pl.multiple_of(group * size, size)
            ref.reshape(ref.shape[0] * size, width)[pl.ds(start + cell, planes, stride=SUB), :] = value

    def planes_and_rows(field, slot, way, places):
        pieces = []
        for group in places:
            for cell in range(0, SUB, 2):
                value = [get_cell(field, group, cell + k) for k in range(2)]
                high, low = halves(jnp.concatenate(value, axis=1))
                value = jnp.concatenate([high, low, high], axis=0)
                value = jnp.dot(depth[way], value, preferred_element_type=jnp.float32)
                pieces += [value[:, :width], value[:, width:]]
        value = split(jnp.concatenate(pieces, axis=0), 1)
        value = jnp.dot(value, rows[way], preferred_element_type=jnp.float32)
        value = value[:, :width] + value[:, width:]
        for at, group in enumerate(places):
            for cell in range(SUB):
                first = (at * SUB + cell) * planes
                set_cell(wide[slot], outer + group, cell, value[first : first + planes])

    inner = cells - 2 * edge

    def lines(ref, plane, first, count):
        return ref[pl.ds(first, count), plane].reshape(count * SUB, width)

    def keep(ref, plane, first, value):
        count = value.shape[0] // SUB
        ref[pl.ds(first, count), plane] = value.reshape(count, SUB, width)

    def along_table(table, count, value):
        value = jnp.dot(table, split(value, 0), preferred_element_type=jnp.float32)
        value = value[:count] + value[count:]
        return value[:, :width], value[:, width:]

    def along_middle(slot, way, plane):
        value = [lines(wide[slot], plane + k, outer, groups) for k in range(2)]
        return along_table(middle[way], inner, jnp.concatenate(value, axis=1))

    def along_ends(slot, way, plane):
        low = lines(wide[slot], plane, 0, 3 * outer)
        high = lines(wide[slot], plane, groups - outer, 3 * outer)
        return along_table(ends[way], edge, jnp.concatenate([low, high], axis=1))

    small = size * width <= 65536
    unroll = 8 if small else 1
    batch = 4 if small else 1

    def filter_places(field, slot, way, places):
        for first in range(0, len(places), batch):
            planes_and_rows(field, slot, way, places[first : first + batch])

    def filter_ends(field, slot, way):
        filter_places(field, slot, way, [*range(outer), *range(groups - outer, groups)])

        @pl.when(line > 0)
        def _():
            edge_copy(slot, False).start()

        @pl.when(line < last)
        def _():
            edge_copy(slot, True).start()

    def filter_middle(field, slot, way):
        count = groups - 2 * outer
        step = batch if count % batch == 0 else 1
        if inner:

            @pl.loop(0, count // step)
            def _(turn):
                first = outer + turn * step
                planes_and_rows(field, slot, way, [first + k for k in range(step)])

    def wait_ends(slot):
        @pl.when(line > 0)
        def _():
            edge_copy(slot, False).wait_send()
            edge_copy(slot, True).wait_recv()

        @pl.when(line < last)
        def _():
            edge_copy(slot, True).wait_send()
            edge_copy(slot, False).wait_recv()

    def out_copy(chunk, target_gy):
        part = pl.ds(chunk * (planes // CHUNKS), planes // CHUNKS)
        return pltpu.make_async_remote_copy(
            src_ref=stage.at[target_gy, part],
            dst_ref=out.at[mine, place % per_gx, part],
            send_sem=out_send.at[chunk, target_gy],
            recv_sem=out_recv.at[chunk, mine, place % per_gx],
            device_id=(pair * 2 + place // per_gx, target_gy),
            device_id_type=MESH,
        )

    def own_copy(chunk):
        part = pl.ds(chunk * (planes // CHUNKS), planes // CHUNKS)
        return pltpu.make_async_copy(
            stage.at[gy, part], out.at[mine, place % per_gx, part], own_sem.at[chunk]
        )

    def is_own(target_gy):
        return jnp.logical_and(target_gy == gy, place // per_gx == core)

    top = groups - outer

    def middle_lines(slot, way, use):
        if inner:

            @pl.loop(0, planes // 2, unroll=max(unroll // 2, 1))
            def _(turn):
                for k, value in enumerate(along_middle(slot, way, 2 * turn)):
                    use(2 * turn + k, value)

    def to_ratio(plane, first, value):
        known = lines(cleaned, plane, first, value.shape[0] // SUB)
        keep(ratio, plane, first, known / (value + BACKGROUND))

    filter_ends(cleaned, 0, 0)
    for iteration in range(ITERS):
        source = cleaned if iteration == 0 else estimate

        def to_estimate(plane, first, value):
            keep(estimate, plane, first, lines(source, plane, first, value.shape[0] // SUB) * value)

        filter_middle(source, 0, 0)
        middle_lines(0, 0, lambda plane, value: to_ratio(plane, outer, value))
        wait_ends(0)

        @pl.loop(0, planes, unroll=unroll)
        def _(plane):
            low, high = along_ends(0, 0, plane)
            to_ratio(plane, 0, low)
            to_ratio(plane, top, high)

        filter_ends(ratio, 1, 1)
        filter_middle(ratio, 1, 1)
        middle_lines(1, 1, lambda plane, value: to_estimate(plane, outer, value))
        wait_ends(1)
        if iteration < ITERS - 1:

            @pl.loop(0, planes, unroll=unroll)
            def _(plane):
                low, high = along_ends(1, 1, plane)
                to_estimate(plane, 0, low)
                to_estimate(plane, top, high)

            filter_ends(estimate, 0, 0)
        else:
            for chunk in range(CHUNKS):

                @pl.loop(chunk * (planes // CHUNKS), (chunk + 1) * (planes // CHUNKS), unroll=unroll)
                def _(plane):
                    low, high = along_ends(1, 1, plane)
                    pieces = [lines(source, plane, 0, outer) * low]
                    if inner:
                        pieces.append(lines(estimate, plane, outer, groups - 2 * outer))
                    pieces.append(lines(source, plane, top, outer) * high)
                    value = jnp.concatenate(pieces, axis=0).T
                    for target in range(count_gy):
                        stage[target, plane] = value[target * lines_x : (target + 1) * lines_x]

                for step in range(count_gy):
                    target = lax.rem(gy + 1 + step, count_gy)

                    @pl.when(is_own(target))
                    def _():
                        own_copy(chunk).start()

                    @pl.when(jnp.logical_not(is_own(target)))
                    def _():
                        out_copy(chunk, target).start()

    for chunk in range(CHUNKS):
        part = pl.ds(chunk * (planes // CHUNKS), planes // CHUNKS)
        for target in range(count_gy):

            @pl.when(is_own(target))
            def _():
                own_copy(chunk).wait()

            @pl.when(jnp.logical_not(is_own(target)))
            def _():
                out_copy(chunk, target).wait_send()

        for channel in range(channels):
            for slot in range(per_gx):
                here = jnp.logical_and(channel == mine, place == core * per_gx + slot)

                @pl.when(jnp.logical_not(here))
                def _():
                    pltpu.make_async_remote_copy(
                        src_ref=stage.at[0, part],
                        dst_ref=out.at[channel, slot, part],
                        send_sem=out_send.at[chunk, 0],
                        recv_sem=out_recv.at[chunk, channel, slot],
                        device_id=(gx, gy),
                        device_id_type=MESH,
                    ).wait_recv()


def local(raw_stack, psf_taps):
    channels, own_planes, lines_x, lines_y = raw_stack.shape
    half_taps = psf_taps.shape[2] // 2
    count_gx = lax.axis_size("gx")
    count_gy = lax.axis_size("gy")
    pairs = count_gx // 2
    cells = lines_y // (pairs * count_gy)
    planes = own_planes * count_gx * count_gy
    edge = -(-half_taps // SUB) * SUB

    block = min(lines_y, 256)
    groups = cells // SUB
    outer = edge // SUB
    per_gx = count_gy // 2
    block_x = lines_x // count_gy
    field = pltpu.VMEM((groups, planes, SUB, lines_x), jnp.float32)
    wide = pltpu.VMEM((groups + 2 * outer, planes, SUB, lines_x), jnp.float32)
    gathered = pl.pallas_call(
        functools.partial(deconvolve_kernel, count_gx, count_gy, edge),
        out_shape=jax.ShapeDtypeStruct((channels, per_gx, planes, block_x, cells), jnp.float32),
        in_specs=[pl.BlockSpec(memory_space=pl.ANY), pl.BlockSpec(memory_space=pltpu.SMEM)],
        out_specs=pl.BlockSpec(memory_space=pl.ANY),
        scratch_shapes=[
            field,
            field,
            field,
            wide,
            wide,
            pltpu.VMEM((planes, groups, SUB, lines_x), jnp.float32),
            pltpu.VMEM((count_gy, planes, block_x, cells), jnp.float32),
            pltpu.VMEM((2 * block, lines_y), jnp.bfloat16),
            pltpu.VMEM((2 * lines_x, lines_y), jnp.bfloat16),
            pltpu.VMEM((2 * lines_x, lines_x), jnp.bfloat16),
            pltpu.VMEM((2, planes, 3 * planes), jnp.bfloat16),
            pltpu.VMEM((2, 2 * lines_x, 2 * lines_x), jnp.bfloat16),
            pltpu.VMEM((2, 2 * max(cells - 2 * edge, edge), 2 * cells), jnp.bfloat16),
            pltpu.VMEM((2, 2 * edge, 6 * edge), jnp.bfloat16),
            pltpu.VMEM((lines_x, lines_y), jnp.float32),
            pltpu.SemaphoreType.DMA((2, 2)),
            pltpu.SemaphoreType.DMA((2, 2)),
            pltpu.SemaphoreType.DMA((CHUNKS, count_gy)),
            pltpu.SemaphoreType.DMA((CHUNKS, channels, per_gx)),
            pltpu.SemaphoreType.DMA((CHUNKS,)),
            pltpu.SemaphoreType.DMA((planes,)),
            pltpu.SemaphoreType.DMA((planes,)),
            pltpu.SemaphoreType.DMA,
        ],
        compiler_params=pltpu.CompilerParams(
            collective_id=0, has_side_effects=True, vmem_limit_bytes=67043328
        ),
    )(raw_stack, psf_taps)
    return jnp.transpose(gathered, (0, 2, 3, 1, 4)).reshape(
        channels, planes, block_x, per_gx * cells
    )


def solution(mesh):
    in_specs = (P(None, ("gx", "gy"), None, None), P())
    out_specs = P(None, None, "gy", "gx")
    return jax.shard_map(local, mesh=mesh, in_specs=in_specs, out_specs=out_specs, check_vma=False)
```

```python
import functools

import jax
import jax.numpy as jnp
from jax import lax
from jax.experimental import pallas as pl
from jax.experimental.pallas import tpu as pltpu
from jax.sharding import PartitionSpec as P

ITERS = 2
BACKGROUND = 0.5
SIGMA_ACROSS = 48.0
SIGMA_ALONG = 96.0
SUB = 8
CHUNKS = 4
PIECES = 4
MESH = pl.DeviceIdType.MESH


def smoothing_table(length_cells, spread_cells):
    rows = lax.broadcasted_iota(jnp.int32, (length_cells, length_cells), 0)
    columns = lax.broadcasted_iota(jnp.int32, (length_cells, length_cells), 1)
    scaled = (rows - columns).astype(jnp.float32) / spread_cells
    kernel_table = jnp.exp(-0.5 * scaled * scaled)
    return kernel_table / jnp.sum(kernel_table, axis=1, keepdims=True)


def circular_row(length_cells, spread_cells):
    places = lax.broadcasted_iota(jnp.int32, (1, length_cells), 1)
    scaled = jnp.minimum(places, length_cells - places).astype(jnp.float32) / spread_cells
    kernel_row = jnp.exp(-0.5 * scaled * scaled)
    return kernel_row / jnp.sum(kernel_row, axis=1, keepdims=True)


def base_rows(taps, axis, channel, reach, lag_of):
    count = taps.shape[2]
    width = -(-2 * reach // 128) * 128
    place = lax.broadcasted_iota(jnp.int32, (1, width), 1)
    lag = lag_of(jnp.where(place < width // 2, place, place - width))
    forward = jnp.zeros((1, width), jnp.float32)
    backward = forward
    total = forward
    for k in range(count):
        tap = taps[axis, channel, k]
        total = total + tap
        forward = jnp.where(lag == k, tap, forward)
        backward = jnp.where(lag == count - 1 - k, tap, backward)
    return forward / total, backward / total


def shifted(base, start, count, columns):
    block = jnp.broadcast_to(base, (count, base.shape[1]))
    block = pltpu.roll(block, start, 1, stride=1, stride_axis=0)[:, :columns]
    high = block.astype(jnp.bfloat16)
    return high, (block - high.astype(jnp.float32)).astype(jnp.bfloat16)


def fill_tables(taps, channel, edge, cells, depth, rows, middle, ends):
    planes, width = depth.shape[1], rows.shape[1] // 2
    half = taps.shape[2] // 2
    depth_base = base_rows(taps, 0, channel, planes, lambda d: d + half)
    rows_base = base_rows(taps, 1, channel, width, lambda d: half - d)
    lines_base = base_rows(taps, 2, channel, max(cells, 3 * edge), lambda d: d - edge + half)
    for way in range(2):
        high, low = shifted(depth_base[way], 0, planes, planes)
        depth[way] = jnp.concatenate([high, high, low], axis=1)
        high, low = shifted(rows_base[way], 0, width, width)
        both = jnp.concatenate([high, low], axis=1)
        rows[way] = jnp.concatenate([both, both], axis=0)
        if cells > 2 * edge:
            high, low = shifted(lines_base[way], 0, cells - 2 * edge, cells)
            middle[way] = twice(high, low)
        high, low = shifted(lines_base[way], 0, edge, 3 * edge)
        ends[way] = twice(high, low)


def twice(high, low):
    both = jnp.concatenate([high, low], axis=0)
    return jnp.concatenate([both, both], axis=1)


def halves(value):
    high = value.astype(jnp.bfloat16)
    return high, (value - high.astype(jnp.float32)).astype(jnp.bfloat16)


def split(value, axis):
    return jnp.concatenate(halves(value), axis=axis)


def turned(count_gy, pair, along):
    odd = pair % 2
    return (1 - odd) * along + odd * (count_gy - 1 - along)


def device_of(count_gy, channels, channel, line):
    pair = line // count_gy
    along = turned(count_gy, pair, line % count_gy)
    return pair * 2 + along % 2, channel * (count_gy // channels) + along // 2


def deconvolve_kernel(
    count_gx, count_gy, edge, raw, taps, out,
    cleaned, estimate, ratio, wide0, wide1, leaving, stage, along, smooth, across, depth, rows, middle, ends,
    held, send_sem, recv_sem, out_send, out_recv, own_sem, plane_send, plane_recv, held_sem,
):
    groups, planes, _, width = cleaned.shape
    cells = groups * SUB
    size = planes * SUB
    wide = (wide0, wide1)
    gx, gy = lax.axis_index("gx"), lax.axis_index("gy")
    pair, core = gx // 2, gx % 2
    channels, _, _, lines_y = raw.shape
    per_channel = count_gy // channels
    mine = gy // per_channel
    place = turned(count_gy, pair, gy % per_channel * 2 + core)
    line = pair * count_gy + place
    last = count_gx // 2 * count_gy - 1
    per_gx = count_gy // 2
    lines_x = width // count_gy
    me = gx * count_gy + gy

    def load(channel):
        return pltpu.make_async_copy(raw.at[channel, 0], held, held_sem)

    def channel_of(turn):
        return lax.rem(turn + core, channels)

    load(channel_of(0)).start()
    barrier = pltpu.get_barrier_semaphore()

    @pl.loop(0, count_gx * count_gy)
    def _(other):
        @pl.when(other != me)
        def _():
            pl.semaphore_signal(
                barrier, inc=1, device_id=(other // count_gy, other % count_gy), device_id_type=MESH
            )

    block = along.shape[0] // 2
    blocks = lines_y // block
    chunks = lines_y // cells
    per_block = block // cells
    table = smoothing_table(width, SIGMA_ACROSS)
    high = table.astype(jnp.bfloat16)
    across[0:width] = high
    across[width : 2 * width] = (table - high.astype(jnp.float32)).astype(jnp.bfloat16)
    high, low = shifted(circular_row(lines_y, SIGMA_ALONG), 0, block, lines_y)
    along[0:block] = high
    along[block : 2 * block] = low

    def smooth_block(index):
        columns = pl.ds(pl.multiple_of(index * block, block), block)
        value = held[:, columns]
        high = value.astype(jnp.bfloat16)
        low = (value - high.astype(jnp.float32)).astype(jnp.bfloat16)
        product = jnp.dot(across[...], high, preferred_element_type=jnp.float32)
        total = product[:width] + product[width:]
        total += jnp.dot(across[0:width], low, preferred_element_type=jnp.float32)
        high = total.astype(jnp.bfloat16)
        smooth[0:width, columns] = high
        smooth[width : 2 * width, columns] = (total - high.astype(jnp.float32)).astype(jnp.bfloat16)

    def clean_block(channel, index):
        total = jnp.zeros((width, block), jnp.float32)
        for other in range(blocks):
            columns = pl.ds(other * block, block)
            shift = lax.rem(index - other + blocks, blocks)
            table = pl.ds(pl.multiple_of(shift * block, block), block)
            product = jnp.dot(
                smooth[:, columns], along[0:block, table], preferred_element_type=jnp.float32
            )
            total += product[:width] + product[width:]
            total += jnp.dot(
                smooth[0:width, columns], along[block : 2 * block, table],
                preferred_element_type=jnp.float32,
            )
        columns = pl.ds(pl.multiple_of(index * block, block), block)
        smoothed = smooth[0:width, columns].astype(jnp.float32)
        smoothed += smooth[width : 2 * width, columns].astype(jnp.float32)
        value = jnp.maximum(held[:, columns] - (smoothed - total), 0.0)
        leaving[pl.ds(channel * chunks + index * per_block, per_block)] = value.T.reshape(
            per_block, groups, SUB, width
        )

    def plane_copy(channel, chunk):
        target_gx, target_gy = device_of(count_gy, channels, channel, chunk)
        return pltpu.make_async_remote_copy(
            src_ref=leaving.at[channel * chunks + chunk],
            dst_ref=cleaned.at[:, me],
            send_sem=plane_send.at[channel * chunks + chunk],
            recv_sem=plane_recv.at[me],
            device_id=(target_gx, target_gy),
            device_id_type=MESH,
        )

    own_plane = pltpu.make_async_copy(
        leaving.at[mine * chunks + line], cleaned.at[:, me], plane_send.at[mine * chunks + line]
    )

    def is_own_plane(channel, chunk):
        return jnp.logical_and(channel == mine, chunk == line)

    for turn in range(channels):
        channel = channel_of(turn)
        if turn > 0:
            load(channel).start()
        load(channel).wait()

        @pl.loop(0, blocks, unroll=2)
        def _(index):
            smooth_block(index)

        if turn == 0:
            pl.semaphore_wait(barrier, count_gx * count_gy - 1)

        @pl.loop(0, blocks)
        def _(step):
            index = lax.rem(step + (line + 1) // per_block + blocks // 2, blocks)
            clean_block(channel, index)
            for part in range(per_block):
                chunk = index * per_block + part

                @pl.when(is_own_plane(channel, chunk))
                def _():
                    own_plane.start()

                @pl.when(jnp.logical_not(is_own_plane(channel, chunk)))
                def _():
                    plane_copy(channel, chunk).start()

    fill_tables(taps, mine, edge, cells, depth, rows, middle, ends)

    outer = edge // SUB
    zeros = jnp.zeros((outer, planes, SUB, width), jnp.float32)

    @pl.when(line == 0)
    def _():
        for slot in range(2):
            wide[slot][0:outer] = zeros

    @pl.when(line == last)
    def _():
        for slot in range(2):
            wide[slot][outer + groups :] = zeros

    own_plane.wait()
    for channel in range(channels):

        @pl.loop(0, chunks)
        def _(chunk):
            @pl.when(jnp.logical_not(is_own_plane(channel, chunk)))
            def _():
                plane_copy(channel, chunk).wait_send()

    @pl.loop(0, count_gx * count_gy)
    def _(other):
        @pl.when(other != me)
        def _():
            pltpu.make_async_remote_copy(
                src_ref=leaving.at[0],
                dst_ref=cleaned.at[:, other],
                send_sem=plane_send.at[0],
                recv_sem=plane_recv.at[other],
                device_id=(gx, gy),
                device_id_type=MESH,
            ).wait_recv()

    per_piece = planes // PIECES

    def edge_copy(slot, up, piece):
        target_gx, target_gy = device_of(count_gy, channels, mine, line + (1 if up else -1))
        source = groups if up else outer
        target = 0 if up else outer + groups
        side = 1 if up else 0
        part = pl.ds(piece * per_piece, per_piece)
        return pltpu.make_async_remote_copy(
            src_ref=wide[slot].at[pl.ds(source, outer), part],
            dst_ref=wide[slot].at[pl.ds(target, outer), part],
            send_sem=send_sem.at[slot, side, piece],
            recv_sem=recv_sem.at[slot, side, piece],
            device_id=(target_gx, target_gy),
            device_id_type=MESH,
        )

    def get_cell(ref, group, cell):
        if width > 128:
            return ref[group, :, cell, :]
        start = pl.multiple_of(group * size, size)
        return ref.reshape(ref.shape[0] * size, width)[pl.ds(start + cell, planes, stride=SUB), :]

    def set_cell(ref, group, cell, value):
        if width > 128:
            ref[group, :, cell, :] = value
        else:
            start = pl.multiple_of(group * size, size)
            ref.reshape(ref.shape[0] * size, width)[pl.ds(start + cell, planes, stride=SUB), :] = value

    def planes_and_rows(field, way, places, put):
        pieces = []
        for group in places:
            for cell in range(0, SUB, 2):
                value = [get_cell(field, group, cell + k) for k in range(2)]
                high, low = halves(jnp.concatenate(value, axis=1))
                value = jnp.concatenate([high, low, high], axis=0)
                value = jnp.dot(depth[way], value, preferred_element_type=jnp.float32)
                pieces += [value[:, :width], value[:, width:]]
        value = split(jnp.concatenate(pieces, axis=0), 1)
        value = jnp.dot(value, rows[way], preferred_element_type=jnp.float32)
        value = value[:, :width] + value[:, width:]
        for at, group in enumerate(places):
            for cell in range(SUB):
                first = (at * SUB + cell) * planes
                put(group, cell, value[first : first + planes])

    inner = cells - 2 * edge

    def lines(ref, plane, first, count):
        return ref[pl.ds(first, count), plane].reshape(count * SUB, width)

    def keep(ref, plane, first, value):
        count = value.shape[0] // SUB
        ref[pl.ds(first, count), plane] = value.reshape(count, SUB, width)

    def along_table(table, count, value):
        value = jnp.dot(table, split(value, 0), preferred_element_type=jnp.float32)
        value = value[:count] + value[count:]
        return value[:, :width], value[:, width:]

    def along_middle(slot, way, plane):
        value = [lines(wide[slot], plane + k, outer, groups) for k in range(2)]
        return along_table(middle[way], inner, jnp.concatenate(value, axis=1))

    def along_ends(slot, way, plane):
        low = lines(wide[slot], plane, 0, 3 * outer)
        high = lines(wide[slot], plane, groups - outer, 3 * outer)
        return along_table(ends[way], edge, jnp.concatenate([low, high], axis=1))

    small = size * width <= 65536
    unroll = 8 if small else 1
    batch = 4 if small else 1

    def filter_ends(field, way, put):
        places = [*range(outer), *range(groups - outer, groups)]
        for first in range(0, len(places), batch):
            planes_and_rows(field, way, places[first : first + batch], put)

    count = groups - 2 * outer
    step = batch if count % batch == 0 else 1
    turns = count // step

    def filter_middle(field, way, put, begin, end):
        if end > begin:

            @pl.loop(begin, end)
            def _(turn):
                first = outer + turn * step
                planes_and_rows(field, way, [first + k for k in range(step)], put)

    def send_ends(slot, piece):
        @pl.when(line > 0)
        def _():
            edge_copy(slot, False, piece).start()

        @pl.when(line < last)
        def _():
            edge_copy(slot, True, piece).start()

    def wait_ends(slot, piece):
        @pl.when(line > 0)
        def _():
            edge_copy(slot, False, piece).wait_send()
            edge_copy(slot, True, piece).wait_recv()

        @pl.when(line < last)
        def _():
            edge_copy(slot, True, piece).wait_send()
            edge_copy(slot, False, piece).wait_recv()

    def out_copy(chunk, target_gy):
        part = pl.ds(chunk * (planes // CHUNKS), planes // CHUNKS)
        return pltpu.make_async_remote_copy(
            src_ref=stage.at[target_gy, part],
            dst_ref=out.at[mine, place % per_gx, part],
            send_sem=out_send.at[chunk, target_gy],
            recv_sem=out_recv.at[chunk, mine, place % per_gx],
            device_id=(pair * 2 + place // per_gx, target_gy),
            device_id_type=MESH,
        )

    def own_copy(chunk):
        part = pl.ds(chunk * (planes // CHUNKS), planes // CHUNKS)
        return pltpu.make_async_copy(
            stage.at[gy, part], out.at[mine, place % per_gx, part], own_sem.at[chunk]
        )

    def is_own(target_gy):
        return jnp.logical_and(target_gy == gy, place // per_gx == core)

    top = groups - outer

    def middle_lines(slot, use):
        if inner:

            @pl.loop(0, planes // 2, unroll=max(unroll // 2, 1))
            def _(turn):
                for k, value in enumerate(along_middle(slot, slot, 2 * turn)):
                    use(2 * turn + k, outer, value)

    def end_lines(slot, piece, use):
        wait_ends(slot, piece)

        @pl.loop(piece * per_piece, (piece + 1) * per_piece, unroll=min(unroll, per_piece))
        def _(plane):
            low, high = along_ends(slot, slot, plane)
            use(plane, 0, low)
            use(plane, top, high)

    def to_ratio(plane, first, value):
        known = lines(cleaned, plane, first, value.shape[0] // SUB)
        keep(wide1, plane, outer + first, known / (value + BACKGROUND))

    def to_blurred(plane, first, value):
        keep(ratio, plane, first, value)

    def to_wide(group, cell, value):
        set_cell(wide0, outer + group, cell, value)

    def forward_ends(source):
        filter_ends(source, 0, to_wide)
        for piece in range(PIECES):
            send_ends(0, piece)

    forward_ends(cleaned)
    for iteration in range(ITERS):
        source = cleaned if iteration == 0 else estimate
        more = iteration < ITERS - 1
        early = max(turns - 1, 0) if more else turns

        def to_estimate(group, cell, value):
            set_cell(estimate, group, cell, get_cell(source, group, cell) * value)

        filter_middle(source, 0, to_wide, 0, turns)
        middle_lines(0, to_ratio)
        for piece in range(PIECES):
            end_lines(0, piece, to_ratio)
            send_ends(1, piece)
        middle_lines(1, to_blurred)
        filter_middle(ratio, 1, to_estimate, 0, early)
        for piece in range(PIECES):
            end_lines(1, piece, to_blurred)
        filter_ends(ratio, 1, to_estimate)
        if more:
            forward_ends(estimate)
        filter_middle(ratio, 1, to_estimate, early, turns)

    for chunk in range(CHUNKS):

        @pl.loop(chunk * (planes // CHUNKS), (chunk + 1) * (planes // CHUNKS), unroll=unroll)
        def _(plane):
            value = lines(estimate, plane, 0, groups).T
            for target in range(count_gy):
                stage[target, plane] = value[target * lines_x : (target + 1) * lines_x]

        for step_gy in range(count_gy):
            target = lax.rem(gy + 1 + step_gy, count_gy)

            @pl.when(is_own(target))
            def _():
                own_copy(chunk).start()

            @pl.when(jnp.logical_not(is_own(target)))
            def _():
                out_copy(chunk, target).start()

    for chunk in range(CHUNKS):
        part = pl.ds(chunk * (planes // CHUNKS), planes // CHUNKS)
        for target in range(count_gy):

            @pl.when(is_own(target))
            def _():
                own_copy(chunk).wait()

            @pl.when(jnp.logical_not(is_own(target)))
            def _():
                out_copy(chunk, target).wait_send()

        for channel in range(channels):
            for slot in range(per_gx):
                here = jnp.logical_and(channel == mine, place == core * per_gx + slot)

                @pl.when(jnp.logical_not(here))
                def _():
                    pltpu.make_async_remote_copy(
                        src_ref=stage.at[0, part],
                        dst_ref=out.at[channel, slot, part],
                        send_sem=out_send.at[chunk, 0],
                        recv_sem=out_recv.at[chunk, channel, slot],
                        device_id=(gx, gy),
                        device_id_type=MESH,
                    ).wait_recv()


def local(raw_stack, psf_taps):
    channels, own_planes, lines_x, lines_y = raw_stack.shape
    half_taps = psf_taps.shape[2] // 2
    count_gx = lax.axis_size("gx")
    count_gy = lax.axis_size("gy")
    pairs = count_gx // 2
    cells = lines_y // (pairs * count_gy)
    planes = own_planes * count_gx * count_gy
    edge = -(-half_taps // SUB) * SUB

    block = min(lines_y, 256)
    groups = cells // SUB
    outer = edge // SUB
    per_gx = count_gy // 2
    block_x = lines_x // count_gy
    field = pltpu.VMEM((groups, planes, SUB, lines_x), jnp.float32)
    wide = pltpu.VMEM((groups + 2 * outer, planes, SUB, lines_x), jnp.float32)
    gathered = pl.pallas_call(
        functools.partial(deconvolve_kernel, count_gx, count_gy, edge),
        out_shape=jax.ShapeDtypeStruct((channels, per_gx, planes, block_x, cells), jnp.float32),
        in_specs=[pl.BlockSpec(memory_space=pl.ANY), pl.BlockSpec(memory_space=pltpu.SMEM)],
        out_specs=pl.BlockSpec(memory_space=pl.ANY),
        scratch_shapes=[
            field,
            field,
            field,
            wide,
            wide,
            pltpu.VMEM((planes, groups, SUB, lines_x), jnp.float32),
            pltpu.VMEM((count_gy, planes, block_x, cells), jnp.float32),
            pltpu.VMEM((2 * block, lines_y), jnp.bfloat16),
            pltpu.VMEM((2 * lines_x, lines_y), jnp.bfloat16),
            pltpu.VMEM((2 * lines_x, lines_x), jnp.bfloat16),
            pltpu.VMEM((2, planes, 3 * planes), jnp.bfloat16),
            pltpu.VMEM((2, 2 * lines_x, 2 * lines_x), jnp.bfloat16),
            pltpu.VMEM((2, 2 * max(cells - 2 * edge, edge), 2 * cells), jnp.bfloat16),
            pltpu.VMEM((2, 2 * edge, 6 * edge), jnp.bfloat16),
            pltpu.VMEM((lines_x, lines_y), jnp.float32),
            pltpu.SemaphoreType.DMA((2, 2, PIECES)),
            pltpu.SemaphoreType.DMA((2, 2, PIECES)),
            pltpu.SemaphoreType.DMA((CHUNKS, count_gy)),
            pltpu.SemaphoreType.DMA((CHUNKS, channels, per_gx)),
            pltpu.SemaphoreType.DMA((CHUNKS,)),
            pltpu.SemaphoreType.DMA((planes,)),
            pltpu.SemaphoreType.DMA((planes,)),
            pltpu.SemaphoreType.DMA,
        ],
        compiler_params=pltpu.CompilerParams(
            collective_id=0, has_side_effects=True, vmem_limit_bytes=67043328
        ),
    )(raw_stack, psf_taps)
    return jnp.transpose(gathered, (0, 2, 3, 1, 4)).reshape(
        channels, planes, block_x, per_gx * cells
    )


def solution(mesh):
    in_specs = (P(None, ("gx", "gy"), None, None), P())
    out_specs = P(None, None, "gy", "gx")
    return jax.shard_map(local, mesh=mesh, in_specs=in_specs, out_specs=out_specs, check_vma=False)
```

```python
import functools

import jax
import jax.numpy as jnp
from jax import lax
from jax.experimental import pallas as pl
from jax.experimental.pallas import tpu as pltpu
from jax.sharding import PartitionSpec as P

ITERS = 2
BACKGROUND = 0.5
SIGMA_ACROSS = 48.0
SIGMA_ALONG = 96.0
SUB = 8
CHUNKS = 4
PIECES = 4
MOVES = 4
MESH = pl.DeviceIdType.MESH


def smoothing_table(length_cells, spread_cells):
    rows = lax.broadcasted_iota(jnp.int32, (length_cells, length_cells), 0)
    columns = lax.broadcasted_iota(jnp.int32, (length_cells, length_cells), 1)
    scaled = (rows - columns).astype(jnp.float32) / spread_cells
    kernel_table = jnp.exp(-0.5 * scaled * scaled)
    return kernel_table / jnp.sum(kernel_table, axis=1, keepdims=True)


def circular_row(length_cells, spread_cells):
    places = lax.broadcasted_iota(jnp.int32, (1, length_cells), 1)
    scaled = jnp.minimum(places, length_cells - places).astype(jnp.float32) / spread_cells
    kernel_row = jnp.exp(-0.5 * scaled * scaled)
    return kernel_row / jnp.sum(kernel_row, axis=1, keepdims=True)


def base_rows(taps, axis, channel, reach, lag_of):
    count = taps.shape[2]
    width = -(-2 * reach // 128) * 128
    place = lax.broadcasted_iota(jnp.int32, (1, width), 1)
    lag = lag_of(jnp.where(place < width // 2, place, place - width))
    forward = jnp.zeros((1, width), jnp.float32)
    backward = forward
    total = forward
    for k in range(count):
        tap = taps[axis, channel, k]
        total = total + tap
        forward = jnp.where(lag == k, tap, forward)
        backward = jnp.where(lag == count - 1 - k, tap, backward)
    return forward / total, backward / total


def shifted(base, start, count, columns):
    block = jnp.broadcast_to(base, (count, base.shape[1]))
    block = pltpu.roll(block, start, 1, stride=1, stride_axis=0)[:, :columns]
    high = block.astype(jnp.bfloat16)
    return high, (block - high.astype(jnp.float32)).astype(jnp.bfloat16)


def fill_tables(taps, channel, edge, cells, depth, rows, middle, ends):
    planes, width = depth.shape[1], rows.shape[1] // 2
    half = taps.shape[2] // 2
    depth_base = base_rows(taps, 0, channel, planes, lambda d: d + half)
    rows_base = base_rows(taps, 1, channel, width, lambda d: half - d)
    lines_base = base_rows(taps, 2, channel, max(cells, 3 * edge), lambda d: d - edge + half)
    for way in range(2):
        high, low = shifted(depth_base[way], 0, planes, planes)
        depth[way] = jnp.concatenate([high, high, low], axis=1)
        high, low = shifted(rows_base[way], 0, width, width)
        both = jnp.concatenate([high, low], axis=1)
        rows[way] = jnp.concatenate([both, both], axis=0)
        if cells > 2 * edge:
            high, low = shifted(lines_base[way], 0, cells - 2 * edge, cells)
            middle[way] = twice(high, low)
        high, low = shifted(lines_base[way], 0, edge, 3 * edge)
        ends[way] = twice(high, low)


def twice(high, low):
    both = jnp.concatenate([high, low], axis=0)
    return jnp.concatenate([both, both], axis=1)


def halves(value):
    high = value.astype(jnp.bfloat16)
    return high, (value - high.astype(jnp.float32)).astype(jnp.bfloat16)


def split(value, axis):
    return jnp.concatenate(halves(value), axis=axis)


def turned(count_gy, pair, along):
    odd = pair % 2
    return (1 - odd) * along + odd * (count_gy - 1 - along)


def device_of(count_gy, channels, channel, line):
    pair = line // count_gy
    along = turned(count_gy, pair, line % count_gy)
    return pair * 2 + along % 2, channel * (count_gy // channels) + along // 2


def deconvolve_kernel(
    count_gx, count_gy, edge, raw, taps, out,
    cleaned, estimate, ratio, wide0, wide1, leaving, stage, along, smooth, across, depth, rows, middle, ends,
    held, send_sem, recv_sem, out_send, out_recv, own_sem, plane_send, plane_recv, held_sem,
):
    groups, planes, _, width = cleaned.shape
    cells = groups * SUB
    size = planes * SUB
    wide = (wide0, wide1)
    gx, gy = lax.axis_index("gx"), lax.axis_index("gy")
    pair, core = gx // 2, gx % 2
    channels, _, _, lines_y = raw.shape
    per_channel = count_gy // channels
    mine = gy // per_channel
    place = turned(count_gy, pair, gy % per_channel * 2 + core)
    line = pair * count_gy + place
    last = count_gx // 2 * count_gy - 1
    per_gx = count_gy // 2
    lines_x = width // count_gy
    me = gx * count_gy + gy

    def load(channel):
        return pltpu.make_async_copy(raw.at[channel, 0], held, held_sem)

    def channel_of(turn):
        return lax.rem(turn + core, channels)

    load(channel_of(0)).start()
    barrier = pltpu.get_barrier_semaphore()

    @pl.loop(0, count_gx * count_gy)
    def _(other):
        @pl.when(other != me)
        def _():
            pl.semaphore_signal(
                barrier, inc=1, device_id=(other // count_gy, other % count_gy), device_id_type=MESH
            )

    block = along.shape[0] // 2
    blocks = lines_y // block
    chunks = lines_y // cells
    per_block = block // cells
    table = smoothing_table(width, SIGMA_ACROSS)
    high = table.astype(jnp.bfloat16)
    across[0:width] = high
    across[width : 2 * width] = (table - high.astype(jnp.float32)).astype(jnp.bfloat16)
    high, low = shifted(circular_row(lines_y, SIGMA_ALONG), 0, block, lines_y)
    along[0:block] = high
    along[block : 2 * block] = low

    def smooth_block(index):
        columns = pl.ds(pl.multiple_of(index * block, block), block)
        value = held[:, columns]
        high = value.astype(jnp.bfloat16)
        low = (value - high.astype(jnp.float32)).astype(jnp.bfloat16)
        product = jnp.dot(across[...], high, preferred_element_type=jnp.float32)
        total = product[:width] + product[width:]
        total += jnp.dot(across[0:width], low, preferred_element_type=jnp.float32)
        high = total.astype(jnp.bfloat16)
        smooth[0:width, columns] = high
        smooth[width : 2 * width, columns] = (total - high.astype(jnp.float32)).astype(jnp.bfloat16)

    def clean_block(channel, index):
        total = jnp.zeros((width, block), jnp.float32)
        for other in range(blocks):
            columns = pl.ds(other * block, block)
            shift = lax.rem(index - other + blocks, blocks)
            table = pl.ds(pl.multiple_of(shift * block, block), block)
            product = jnp.dot(
                smooth[:, columns], along[0:block, table], preferred_element_type=jnp.float32
            )
            total += product[:width] + product[width:]
            total += jnp.dot(
                smooth[0:width, columns], along[block : 2 * block, table],
                preferred_element_type=jnp.float32,
            )
        columns = pl.ds(pl.multiple_of(index * block, block), block)
        smoothed = smooth[0:width, columns].astype(jnp.float32)
        smoothed += smooth[width : 2 * width, columns].astype(jnp.float32)
        value = jnp.maximum(held[:, columns] - (smoothed - total), 0.0)
        leaving[pl.ds(channel * chunks + index * per_block, per_block)] = value.T.reshape(
            per_block, groups, SUB, width
        )

    def plane_copy(channel, chunk):
        target_gx, target_gy = device_of(count_gy, channels, channel, chunk)
        return pltpu.make_async_remote_copy(
            src_ref=leaving.at[channel * chunks + chunk],
            dst_ref=cleaned.at[:, me],
            send_sem=plane_send.at[channel * chunks + chunk],
            recv_sem=plane_recv.at[me],
            device_id=(target_gx, target_gy),
            device_id_type=MESH,
        )

    own_plane = pltpu.make_async_copy(
        leaving.at[mine * chunks + line], cleaned.at[:, me], plane_send.at[mine * chunks + line]
    )

    def is_own_plane(channel, chunk):
        return jnp.logical_and(channel == mine, chunk == line)

    for turn in range(channels):
        channel = channel_of(turn)
        if turn > 0:
            load(channel).start()
        load(channel).wait()

        @pl.loop(0, blocks, unroll=2)
        def _(index):
            smooth_block(index)

        if turn == 0:
            pl.semaphore_wait(barrier, count_gx * count_gy - 1)

        @pl.loop(0, blocks)
        def _(step):
            index = lax.rem(step + (line + 1) // per_block + blocks // 2, blocks)
            clean_block(channel, index)
            for part in range(per_block):
                chunk = index * per_block + part

                @pl.when(is_own_plane(channel, chunk))
                def _():
                    own_plane.start()

                @pl.when(jnp.logical_not(is_own_plane(channel, chunk)))
                def _():
                    plane_copy(channel, chunk).start()

    fill_tables(taps, mine, edge, cells, depth, rows, middle, ends)

    outer = edge // SUB
    zeros = jnp.zeros((outer, planes, SUB, width), jnp.float32)

    @pl.when(line == 0)
    def _():
        for slot in range(2):
            wide[slot][0:outer] = zeros

    @pl.when(line == last)
    def _():
        for slot in range(2):
            wide[slot][outer + groups :] = zeros

    own_plane.wait()
    for channel in range(channels):

        @pl.loop(0, chunks)
        def _(chunk):
            @pl.when(jnp.logical_not(is_own_plane(channel, chunk)))
            def _():
                plane_copy(channel, chunk).wait_send()

    @pl.loop(0, count_gx * count_gy)
    def _(other):
        @pl.when(other != me)
        def _():
            pltpu.make_async_remote_copy(
                src_ref=leaving.at[0],
                dst_ref=cleaned.at[:, other],
                send_sem=plane_send.at[0],
                recv_sem=plane_recv.at[other],
                device_id=(gx, gy),
                device_id_type=MESH,
            ).wait_recv()

    per_piece = planes // PIECES

    def edge_copy(slot, up, piece):
        target_gx, target_gy = device_of(count_gy, channels, mine, line + (1 if up else -1))
        source = groups if up else outer
        target = 0 if up else outer + groups
        side = 1 if up else 0
        part = pl.ds(piece * per_piece, per_piece)
        return pltpu.make_async_remote_copy(
            src_ref=wide[slot].at[pl.ds(source, outer), part],
            dst_ref=wide[slot].at[pl.ds(target, outer), part],
            send_sem=send_sem.at[slot, side, piece],
            recv_sem=recv_sem.at[slot, side, piece],
            device_id=(target_gx, target_gy),
            device_id_type=MESH,
        )

    def get_cell(ref, group, cell):
        if width > 128:
            return ref[group, :, cell, :]
        start = pl.multiple_of(group * size, size)
        return ref.reshape(ref.shape[0] * size, width)[pl.ds(start + cell, planes, stride=SUB), :]

    def set_cell(ref, group, cell, value):
        if width > 128:
            ref[group, :, cell, :] = value
        else:
            start = pl.multiple_of(group * size, size)
            ref.reshape(ref.shape[0] * size, width)[pl.ds(start + cell, planes, stride=SUB), :] = value

    def planes_and_rows(field, way, places, put):
        pieces = []
        for group in places:
            for cell in range(0, SUB, 2):
                value = [get_cell(field, group, cell + k) for k in range(2)]
                high, low = halves(jnp.concatenate(value, axis=1))
                value = jnp.concatenate([high, low, high], axis=0)
                value = jnp.dot(depth[way], value, preferred_element_type=jnp.float32)
                pieces += [value[:, :width], value[:, width:]]
        value = split(jnp.concatenate(pieces, axis=0), 1)
        value = jnp.dot(value, rows[way], preferred_element_type=jnp.float32)
        value = value[:, :width] + value[:, width:]
        for at, group in enumerate(places):
            for cell in range(SUB):
                first = (at * SUB + cell) * planes
                put(group, cell, value[first : first + planes])

    inner = cells - 2 * edge

    def lines(ref, plane, first, count):
        return ref[pl.ds(first, count), plane].reshape(count * SUB, width)

    def keep(ref, plane, first, value):
        count = value.shape[0] // SUB
        ref[pl.ds(first, count), plane] = value.reshape(count, SUB, width)

    def along_table(table, count, value):
        value = jnp.dot(table, split(value, 0), preferred_element_type=jnp.float32)
        value = value[:count] + value[count:]
        return value[:, :width], value[:, width:]

    def along_middle(slot, way, plane):
        value = [lines(wide[slot], plane + k, outer, groups) for k in range(2)]
        return along_table(middle[way], inner, jnp.concatenate(value, axis=1))

    def along_ends(slot, way, plane):
        low = lines(wide[slot], plane, 0, 3 * outer)
        high = lines(wide[slot], plane, groups - outer, 3 * outer)
        return along_table(ends[way], edge, jnp.concatenate([low, high], axis=1))

    small = size * width <= 65536
    unroll = 8 if small else 1
    batch = 4 if small else 1

    def filter_ends(field, way, put):
        places = [*range(outer), *range(groups - outer, groups)]
        for first in range(0, len(places), batch):
            planes_and_rows(field, way, places[first : first + batch], put)

    count = groups - 2 * outer
    step = batch if count % batch == 0 else 1
    turns = count // step

    def filter_middle(field, way, put, begin, end):
        if end > begin:

            @pl.loop(begin, end)
            def _(turn):
                first = outer + turn * step
                planes_and_rows(field, way, [first + k for k in range(step)], put)

    def send_ends(slot, piece):
        @pl.when(line > 0)
        def _():
            edge_copy(slot, False, piece).start()

        @pl.when(line < last)
        def _():
            edge_copy(slot, True, piece).start()

    def wait_ends(slot, piece):
        @pl.when(line > 0)
        def _():
            edge_copy(slot, False, piece).wait_send()
            edge_copy(slot, True, piece).wait_recv()

        @pl.when(line < last)
        def _():
            edge_copy(slot, True, piece).wait_send()
            edge_copy(slot, False, piece).wait_recv()

    def landing(channel, slot, part):
        if cells % 128:
            return out.at[channel, slot, part]
        return out.at[channel, part, :, pl.ds(pl.multiple_of(slot * cells, cells), cells)]

    def out_copy(chunk, target_gy):
        part = pl.ds(chunk * (planes // CHUNKS), planes // CHUNKS)
        return pltpu.make_async_remote_copy(
            src_ref=stage.at[target_gy, part],
            dst_ref=landing(mine, place % per_gx, part),
            send_sem=out_send.at[chunk, target_gy],
            recv_sem=out_recv.at[chunk, mine, place % per_gx],
            device_id=(pair * 2 + place // per_gx, target_gy),
            device_id_type=MESH,
        )

    def own_copy(chunk):
        part = pl.ds(chunk * (planes // CHUNKS), planes // CHUNKS)
        return pltpu.make_async_copy(
            stage.at[gy, part], landing(mine, place % per_gx, part), own_sem.at[chunk]
        )

    def is_own(target_gy):
        return jnp.logical_and(target_gy == gy, place // per_gx == core)

    top = groups - outer

    def middle_lines(slot, use):
        if inner:

            @pl.loop(0, planes // 2, unroll=max(unroll // 2, 1))
            def _(turn):
                for k, value in enumerate(along_middle(slot, slot, 2 * turn)):
                    use(2 * turn + k, outer, value)

    def end_lines(slot, piece, use):
        wait_ends(slot, piece)

        @pl.loop(piece * per_piece, (piece + 1) * per_piece, unroll=min(unroll, per_piece))
        def _(plane):
            low, high = along_ends(slot, slot, plane)
            use(plane, 0, low)
            use(plane, top, high)

    def to_ratio(plane, first, value):
        known = lines(cleaned, plane, first, value.shape[0] // SUB)
        keep(wide1, plane, outer + first, known / (value + BACKGROUND))

    def to_blurred(plane, first, value):
        keep(ratio, plane, first, value)

    def to_wide(group, cell, value):
        set_cell(wide0, outer + group, cell, value)

    def forward_ends(source):
        filter_ends(source, 0, to_wide)
        for piece in range(PIECES):
            send_ends(0, piece)

    forward_ends(cleaned)
    for iteration in range(ITERS):
        source = cleaned if iteration == 0 else estimate
        more = iteration < ITERS - 1
        early = max(turns - 1, 0) if more else turns

        def to_estimate(group, cell, value):
            set_cell(estimate, group, cell, get_cell(source, group, cell) * value)

        filter_middle(source, 0, to_wide, 0, turns)
        middle_lines(0, to_ratio)
        for piece in range(PIECES):
            end_lines(0, piece, to_ratio)
            send_ends(1, piece)
        middle_lines(1, to_blurred)
        filter_middle(ratio, 1, to_estimate, 0, early)
        for piece in range(PIECES):
            end_lines(1, piece, to_blurred)
        filter_ends(ratio, 1, to_estimate)
        if more:
            forward_ends(estimate)
        filter_middle(ratio, 1, to_estimate, early, turns)

    for chunk in range(CHUNKS):

        @pl.loop(chunk * (planes // CHUNKS), (chunk + 1) * (planes // CHUNKS), unroll=unroll)
        def _(plane):
            value = lines(estimate, plane, 0, groups).T
            for target in range(count_gy):
                stage[target, plane] = value[target * lines_x : (target + 1) * lines_x]

        for step_gy in range(count_gy):
            target = lax.rem(gy + 1 + step_gy, count_gy)

            @pl.when(is_own(target))
            def _():
                own_copy(chunk).start()

            @pl.when(jnp.logical_not(is_own(target)))
            def _():
                out_copy(chunk, target).start()

    for chunk in range(CHUNKS):
        part = pl.ds(chunk * (planes // CHUNKS), planes // CHUNKS)
        for target in range(count_gy):

            @pl.when(is_own(target))
            def _():
                own_copy(chunk).wait()

            @pl.when(jnp.logical_not(is_own(target)))
            def _():
                out_copy(chunk, target).wait_send()

        for channel in range(channels):
            for slot in range(per_gx):
                here = jnp.logical_and(channel == mine, place == core * per_gx + slot)

                @pl.when(jnp.logical_not(here))
                def _():
                    pltpu.make_async_remote_copy(
                        src_ref=stage.at[0, part],
                        dst_ref=landing(channel, slot, part),
                        send_sem=out_send.at[chunk, 0],
                        recv_sem=out_recv.at[chunk, channel, slot],
                        device_id=(gx, gy),
                        device_id_type=MESH,
                    ).wait_recv()


def hand_over(source, target, held, load_sem, store_sem):
    channels, planes = source.shape[:2]
    part = planes // MOVES
    spots = [(channel, pl.ds(move * part, part)) for channel in range(channels) for move in range(MOVES)]

    def load(index):
        spot = spots[index]
        return pltpu.make_async_copy(source.at[spot], held.at[spot], load_sem.at[index])

    def store(index):
        spot = spots[index]
        return pltpu.make_async_copy(held.at[spot], target.at[spot], store_sem.at[index])

    for index in range(len(spots)):
        load(index).start()
    for index in range(len(spots)):
        load(index).wait()
        store(index).start()
    for index in range(len(spots)):
        store(index).wait()


def local(raw_stack, psf_taps):
    channels, own_planes, lines_x, lines_y = raw_stack.shape
    half_taps = psf_taps.shape[2] // 2
    count_gx = lax.axis_size("gx")
    count_gy = lax.axis_size("gy")
    pairs = count_gx // 2
    cells = lines_y // (pairs * count_gy)
    planes = own_planes * count_gx * count_gy
    edge = -(-half_taps // SUB) * SUB

    block = min(lines_y, 256)
    groups = cells // SUB
    outer = edge // SUB
    per_gx = count_gy // 2
    block_x = lines_x // count_gy
    field = pltpu.VMEM((groups, planes, SUB, lines_x), jnp.float32)
    wide = pltpu.VMEM((groups + 2 * outer, planes, SUB, lines_x), jnp.float32)
    shape = (channels, planes, block_x, per_gx * cells)
    if cells % 128:
        shape = (channels, per_gx, planes, block_x, cells)
    gathered = pl.pallas_call(
        functools.partial(deconvolve_kernel, count_gx, count_gy, edge),
        out_shape=jax.ShapeDtypeStruct(shape, jnp.float32),
        in_specs=[pl.BlockSpec(memory_space=pl.ANY), pl.BlockSpec(memory_space=pltpu.SMEM)],
        out_specs=pl.BlockSpec(memory_space=pl.ANY),
        scratch_shapes=[
            field,
            field,
            field,
            wide,
            wide,
            pltpu.VMEM((planes, groups, SUB, lines_x), jnp.float32),
            pltpu.VMEM((count_gy, planes, block_x, cells), jnp.float32),
            pltpu.VMEM((2 * block, lines_y), jnp.bfloat16),
            pltpu.VMEM((2 * lines_x, lines_y), jnp.bfloat16),
            pltpu.VMEM((2 * lines_x, lines_x), jnp.bfloat16),
            pltpu.VMEM((2, planes, 3 * planes), jnp.bfloat16),
            pltpu.VMEM((2, 2 * lines_x, 2 * lines_x), jnp.bfloat16),
            pltpu.VMEM((2, 2 * max(cells - 2 * edge, edge), 2 * cells), jnp.bfloat16),
            pltpu.VMEM((2, 2 * edge, 6 * edge), jnp.bfloat16),
            pltpu.VMEM((lines_x, lines_y), jnp.float32),
            pltpu.SemaphoreType.DMA((2, 2, PIECES)),
            pltpu.SemaphoreType.DMA((2, 2, PIECES)),
            pltpu.SemaphoreType.DMA((CHUNKS, count_gy)),
            pltpu.SemaphoreType.DMA((CHUNKS, channels, per_gx)),
            pltpu.SemaphoreType.DMA((CHUNKS,)),
            pltpu.SemaphoreType.DMA((planes,)),
            pltpu.SemaphoreType.DMA((planes,)),
            pltpu.SemaphoreType.DMA,
        ],
        compiler_params=pltpu.CompilerParams(
            collective_id=0, has_side_effects=True, vmem_limit_bytes=67043328
        ),
    )(raw_stack, psf_taps)
    if cells % 128:
        gathered = jnp.transpose(gathered, (0, 2, 3, 1, 4))
        return gathered.reshape(channels, planes, block_x, per_gx * cells)
    return pl.pallas_call(
        hand_over,
        out_shape=jax.ShapeDtypeStruct(shape, jnp.float32),
        in_specs=[pl.BlockSpec(memory_space=pl.ANY)],
        out_specs=pl.BlockSpec(memory_space=pl.ANY),
        scratch_shapes=[
            pltpu.VMEM(shape, jnp.float32),
            pltpu.SemaphoreType.DMA((channels * MOVES,)),
            pltpu.SemaphoreType.DMA((channels * MOVES,)),
        ],
        compiler_params=pltpu.CompilerParams(vmem_limit_bytes=67043328),
    )(gathered)


def solution(mesh):
    in_specs = (P(None, ("gx", "gy"), None, None), P())
    out_specs = P(None, None, "gy", "gx")
    return jax.shard_map(local, mesh=mesh, in_specs=in_specs, out_specs=out_specs, check_vma=False)
```

```python
import functools

import jax
import jax.numpy as jnp
from jax import lax
from jax.experimental import pallas as pl
from jax.experimental.pallas import tpu as pltpu
from jax.sharding import PartitionSpec as P

ITERS = 2
BACKGROUND = 0.5
SIGMA_ACROSS = 48.0
SIGMA_ALONG = 96.0
SUB = 8
CHUNKS = 4
PIECES = 4
MOVES = 4
AHEAD = 1
MESH = pl.DeviceIdType.MESH


def smoothing_table(length_cells, spread_cells):
    rows = lax.broadcasted_iota(jnp.int32, (length_cells, length_cells), 0)
    columns = lax.broadcasted_iota(jnp.int32, (length_cells, length_cells), 1)
    scaled = (rows - columns).astype(jnp.float32) / spread_cells
    kernel_table = jnp.exp(-0.5 * scaled * scaled)
    return kernel_table / jnp.sum(kernel_table, axis=1, keepdims=True)


def circular_row(length_cells, spread_cells):
    places = lax.broadcasted_iota(jnp.int32, (1, length_cells), 1)
    scaled = jnp.minimum(places, length_cells - places).astype(jnp.float32) / spread_cells
    kernel_row = jnp.exp(-0.5 * scaled * scaled)
    return kernel_row / jnp.sum(kernel_row, axis=1, keepdims=True)


def base_rows(taps, axis, channel, reach, lag_of):
    count = taps.shape[2]
    width = -(-2 * reach // 128) * 128
    place = lax.broadcasted_iota(jnp.int32, (1, width), 1)
    lag = lag_of(jnp.where(place < width // 2, place, place - width))
    forward = jnp.zeros((1, width), jnp.float32)
    backward = forward
    total = forward
    for k in range(count):
        tap = taps[axis, channel, k]
        total = total + tap
        forward = jnp.where(lag == k, tap, forward)
        backward = jnp.where(lag == count - 1 - k, tap, backward)
    return forward / total, backward / total


def shifted(base, start, count, columns):
    block = jnp.broadcast_to(base, (count, base.shape[1]))
    block = pltpu.roll(block, start, 1, stride=1, stride_axis=0)[:, :columns]
    high = block.astype(jnp.bfloat16)
    return high, (block - high.astype(jnp.float32)).astype(jnp.bfloat16)


def fill_tables(taps, channel, edge, cells, depth, rows, middle, ends):
    planes, width = depth.shape[1], rows.shape[1] // 2
    half = taps.shape[2] // 2
    depth_base = base_rows(taps, 0, channel, planes, lambda d: d + half)
    rows_base = base_rows(taps, 1, channel, width, lambda d: half - d)
    lines_base = base_rows(taps, 2, channel, max(cells, 3 * edge), lambda d: d - edge + half)
    for way in range(2):
        high, low = shifted(depth_base[way], 0, planes, planes)
        depth[way] = jnp.concatenate([high, high, low], axis=1)
        high, low = shifted(rows_base[way], 0, width, width)
        both = jnp.concatenate([high, low], axis=1)
        rows[way] = jnp.concatenate([both, both], axis=0)
        if cells > 2 * edge:
            high, low = shifted(lines_base[way], 0, cells - 2 * edge, cells)
            middle[way] = twice(high, low)
        high, low = shifted(lines_base[way], 0, edge, 3 * edge)
        ends[way] = twice(high, low)


def twice(high, low):
    both = jnp.concatenate([high, low], axis=0)
    return jnp.concatenate([both, both], axis=1)


def halves(value):
    high = value.astype(jnp.bfloat16)
    return high, (value - high.astype(jnp.float32)).astype(jnp.bfloat16)


def split(value, axis):
    return jnp.concatenate(halves(value), axis=axis)


def turned(count_gy, pair, along):
    odd = pair % 2
    return (1 - odd) * along + odd * (count_gy - 1 - along)


def device_of(count_gy, channels, channel, line):
    pair = line // count_gy
    along = turned(count_gy, pair, line % count_gy)
    return pair * 2 + along % 2, channel * (count_gy // channels) + along // 2


def deconvolve_kernel(
    count_gx, count_gy, edge, raw, taps, out,
    cleaned, estimate, ratio, wide0, wide1, leaving, stage, along, smooth, across, depth, rows, middle, ends,
    held, send_sem, recv_sem, out_send, out_recv, own_sem, plane_send, plane_recv, held_sem,
):
    groups, planes, _, width = cleaned.shape
    cells = groups * SUB
    size = planes * SUB
    wide = (wide0, wide1)
    gx, gy = lax.axis_index("gx"), lax.axis_index("gy")
    pair, core = gx // 2, gx % 2
    channels, _, _, lines_y = raw.shape
    per_channel = count_gy // channels
    mine = gy // per_channel
    place = turned(count_gy, pair, gy % per_channel * 2 + core)
    line = pair * count_gy + place
    last = count_gx // 2 * count_gy - 1
    per_gx = count_gy // 2
    lines_x = width // count_gy
    me = gx * count_gy + gy

    def block_at(step):
        return lax.rem(step + (line + 1) // per_block + blocks // 2, blocks)

    def load(channel):
        return pltpu.make_async_copy(raw.at[channel, 0], held, held_sem)

    def channel_of(turn):
        return lax.rem(turn + core, channels)

    load(channel_of(0)).start()
    barrier = pltpu.get_barrier_semaphore()

    low = 1 - pair * 2 // (count_gx // 2)

    @pl.loop(0, count_gx * count_gy)
    def _(turn):
        other = low * (count_gx * count_gy - 1 - turn) + (1 - low) * turn

        @pl.when(other != me)
        def _():
            pl.semaphore_signal(
                barrier, inc=1, device_id=(other // count_gy, other % count_gy), device_id_type=MESH
            )

    block = along.shape[0] // 2
    blocks = lines_y // block
    chunks = lines_y // cells
    per_block = block // cells
    table = smoothing_table(width, SIGMA_ACROSS)
    high = table.astype(jnp.bfloat16)
    across[0:width] = high
    across[width : 2 * width] = (table - high.astype(jnp.float32)).astype(jnp.bfloat16)
    high, low = shifted(circular_row(lines_y, SIGMA_ALONG), 0, block, lines_y)
    along[0:block] = high
    along[block : 2 * block] = low

    def smooth_block(index):
        columns = pl.ds(pl.multiple_of(index * block, block), block)
        value = held[:, columns]
        high = value.astype(jnp.bfloat16)
        low = (value - high.astype(jnp.float32)).astype(jnp.bfloat16)
        product = jnp.dot(across[...], high, preferred_element_type=jnp.float32)
        total = product[:width] + product[width:]
        total += jnp.dot(across[0:width], low, preferred_element_type=jnp.float32)
        high = total.astype(jnp.bfloat16)
        smooth[0:width, columns] = high
        smooth[width : 2 * width, columns] = (total - high.astype(jnp.float32)).astype(jnp.bfloat16)

    def clean_block(channel, index):
        total = jnp.zeros((width, block), jnp.float32)
        for other in range(blocks):
            columns = pl.ds(other * block, block)
            shift = lax.rem(index - other + blocks, blocks)
            table = pl.ds(pl.multiple_of(shift * block, block), block)
            product = jnp.dot(
                smooth[:, columns], along[0:block, table], preferred_element_type=jnp.float32
            )
            total += product[:width] + product[width:]
            total += jnp.dot(
                smooth[0:width, columns], along[block : 2 * block, table],
                preferred_element_type=jnp.float32,
            )
        columns = pl.ds(pl.multiple_of(index * block, block), block)
        smoothed = smooth[0:width, columns].astype(jnp.float32)
        smoothed += smooth[width : 2 * width, columns].astype(jnp.float32)
        value = jnp.maximum(held[:, columns] - (smoothed - total), 0.0)
        leaving[pl.ds(channel * chunks + index * per_block, per_block)] = value.T.reshape(
            per_block, groups, SUB, width
        )

    def plane_copy(channel, chunk):
        target_gx, target_gy = device_of(count_gy, channels, channel, chunk)
        return pltpu.make_async_remote_copy(
            src_ref=leaving.at[channel * chunks + chunk],
            dst_ref=cleaned.at[:, me],
            send_sem=plane_send.at[channel * chunks + chunk],
            recv_sem=plane_recv.at[me],
            device_id=(target_gx, target_gy),
            device_id_type=MESH,
        )

    own_plane = pltpu.make_async_copy(
        leaving.at[mine * chunks + line], cleaned.at[:, me], plane_send.at[mine * chunks + line]
    )

    def is_own_plane(channel, chunk):
        return jnp.logical_and(channel == mine, chunk == line)

    for turn in range(channels):
        channel = channel_of(turn)
        if turn > 0:
            load(channel).start()
        load(channel).wait()

        @pl.loop(0, blocks, unroll=2)
        def _(index):
            smooth_block(index)

        def send_block(step):
            for part in range(per_block):
                chunk = block_at(step) * per_block + part

                @pl.when(is_own_plane(channel, chunk))
                def _():
                    own_plane.start()

                @pl.when(jnp.logical_not(is_own_plane(channel, chunk)))
                def _():
                    plane_copy(channel, chunk).start()

        ahead = 0
        if turn == 0:
            ahead = min(AHEAD, blocks)

            @pl.loop(0, ahead)
            def _(step):
                clean_block(channel, block_at(step))

            pl.semaphore_wait(barrier, count_gx * count_gy - 1)

            @pl.loop(0, ahead)
            def _(step):
                send_block(step)

        @pl.loop(ahead, blocks)
        def _(step):
            clean_block(channel, block_at(step))
            send_block(step)

    fill_tables(taps, mine, edge, cells, depth, rows, middle, ends)

    outer = edge // SUB
    zeros = jnp.zeros((outer, planes, SUB, width), jnp.float32)

    @pl.when(line == 0)
    def _():
        for slot in range(2):
            wide[slot][0:outer] = zeros

    @pl.when(line == last)
    def _():
        for slot in range(2):
            wide[slot][outer + groups :] = zeros

    own_plane.wait()
    @pl.loop(0, count_gx * count_gy)
    def _(other):
        @pl.when(other != me)
        def _():
            pltpu.make_async_remote_copy(
                src_ref=leaving.at[0],
                dst_ref=cleaned.at[:, other],
                send_sem=plane_send.at[0],
                recv_sem=plane_recv.at[other],
                device_id=(gx, gy),
                device_id_type=MESH,
            ).wait_recv()

    per_piece = planes // PIECES

    def edge_copy(slot, up, piece):
        target_gx, target_gy = device_of(count_gy, channels, mine, line + (1 if up else -1))
        source = groups if up else outer
        target = 0 if up else outer + groups
        side = 1 if up else 0
        part = pl.ds(piece * per_piece, per_piece)
        return pltpu.make_async_remote_copy(
            src_ref=wide[slot].at[pl.ds(source, outer), part],
            dst_ref=wide[slot].at[pl.ds(target, outer), part],
            send_sem=send_sem.at[slot, side, piece],
            recv_sem=recv_sem.at[slot, side, piece],
            device_id=(target_gx, target_gy),
            device_id_type=MESH,
        )

    def get_cell(ref, group, cell):
        if width > 128:
            return ref[group, :, cell, :]
        start = pl.multiple_of(group * size, size)
        return ref.reshape(ref.shape[0] * size, width)[pl.ds(start + cell, planes, stride=SUB), :]

    def set_cell(ref, group, cell, value):
        if width > 128:
            ref[group, :, cell, :] = value
        else:
            start = pl.multiple_of(group * size, size)
            ref.reshape(ref.shape[0] * size, width)[pl.ds(start + cell, planes, stride=SUB), :] = value

    def planes_and_rows(field, way, places, put):
        pieces = []
        for group in places:
            for cell in range(0, SUB, 2):
                value = [get_cell(field, group, cell + k) for k in range(2)]
                high, low = halves(jnp.concatenate(value, axis=1))
                value = jnp.concatenate([high, low, high], axis=0)
                value = jnp.dot(depth[way], value, preferred_element_type=jnp.float32)
                pieces += [value[:, :width], value[:, width:]]
        value = split(jnp.concatenate(pieces, axis=0), 1)
        value = jnp.dot(value, rows[way], preferred_element_type=jnp.float32)
        value = value[:, :width] + value[:, width:]
        for at, group in enumerate(places):
            for cell in range(SUB):
                first = (at * SUB + cell) * planes
                put(group, cell, value[first : first + planes])

    inner = cells - 2 * edge

    def lines(ref, plane, first, count):
        return ref[pl.ds(first, count), plane].reshape(count * SUB, width)

    def keep(ref, plane, first, value):
        count = value.shape[0] // SUB
        ref[pl.ds(first, count), plane] = value.reshape(count, SUB, width)

    def along_table(table, count, value):
        value = jnp.dot(table, split(value, 0), preferred_element_type=jnp.float32)
        value = value[:count] + value[count:]
        return value[:, :width], value[:, width:]

    def along_middle(slot, way, plane):
        value = [lines(wide[slot], plane + k, outer, groups) for k in range(2)]
        return along_table(middle[way], inner, jnp.concatenate(value, axis=1))

    def along_ends(slot, way, plane):
        low = lines(wide[slot], plane, 0, 3 * outer)
        high = lines(wide[slot], plane, groups - outer, 3 * outer)
        return along_table(ends[way], edge, jnp.concatenate([low, high], axis=1))

    small = size * width <= 65536
    unroll = 8 if small else 1
    batch = 4 if small else 1

    def filter_ends(field, way, put):
        places = [*range(outer), *range(groups - outer, groups)]
        for first in range(0, len(places), batch):
            planes_and_rows(field, way, places[first : first + batch], put)

    count = groups - 2 * outer
    step = batch if count % batch == 0 else 1
    turns = count // step

    def filter_middle(field, way, put, begin, end):
        if end > begin:

            @pl.loop(begin, end)
            def _(turn):
                first = outer + turn * step
                planes_and_rows(field, way, [first + k for k in range(step)], put)

    def send_ends(slot, piece):
        @pl.when(line > 0)
        def _():
            edge_copy(slot, False, piece).start()

        @pl.when(line < last)
        def _():
            edge_copy(slot, True, piece).start()

    def wait_ends(slot, piece):
        @pl.when(line > 0)
        def _():
            edge_copy(slot, False, piece).wait_send()
            edge_copy(slot, True, piece).wait_recv()

        @pl.when(line < last)
        def _():
            edge_copy(slot, True, piece).wait_send()
            edge_copy(slot, False, piece).wait_recv()

    def landing(channel, slot, part):
        if cells % 128:
            return out.at[channel, slot, part]
        return out.at[channel, part, :, pl.ds(pl.multiple_of(slot * cells, cells), cells)]

    def out_copy(chunk, target_gy):
        part = pl.ds(chunk * (planes // CHUNKS), planes // CHUNKS)
        return pltpu.make_async_remote_copy(
            src_ref=stage.at[target_gy, part],
            dst_ref=landing(mine, place % per_gx, part),
            send_sem=out_send.at[chunk, target_gy],
            recv_sem=out_recv.at[chunk, mine, place % per_gx],
            device_id=(pair * 2 + place // per_gx, target_gy),
            device_id_type=MESH,
        )

    def own_copy(chunk):
        part = pl.ds(chunk * (planes // CHUNKS), planes // CHUNKS)
        return pltpu.make_async_copy(
            stage.at[gy, part], landing(mine, place % per_gx, part), own_sem.at[chunk]
        )

    def is_own(target_gy):
        return jnp.logical_and(target_gy == gy, place // per_gx == core)

    top = groups - outer

    def middle_lines(slot, use):
        if inner:

            @pl.loop(0, planes // 2, unroll=max(unroll // 2, 1))
            def _(turn):
                for k, value in enumerate(along_middle(slot, slot, 2 * turn)):
                    use(2 * turn + k, outer, value)

    def end_lines(slot, piece, use):
        wait_ends(slot, piece)

        @pl.loop(piece * per_piece, (piece + 1) * per_piece, unroll=min(unroll, per_piece))
        def _(plane):
            low, high = along_ends(slot, slot, plane)
            use(plane, 0, low)
            use(plane, top, high)

    def to_ratio(plane, first, value):
        known = lines(cleaned, plane, first, value.shape[0] // SUB)
        keep(wide1, plane, outer + first, known / (value + BACKGROUND))

    def to_blurred(plane, first, value):
        keep(ratio, plane, first, value)

    def to_wide(group, cell, value):
        set_cell(wide0, outer + group, cell, value)

    def forward_ends(source):
        filter_ends(source, 0, to_wide)
        for piece in range(PIECES):
            send_ends(0, piece)

    forward_ends(cleaned)
    for iteration in range(ITERS):
        source = cleaned if iteration == 0 else estimate
        more = iteration < ITERS - 1
        early = max(turns - 1, 0) if more else turns

        def to_estimate(group, cell, value):
            set_cell(estimate, group, cell, get_cell(source, group, cell) * value)

        filter_middle(source, 0, to_wide, 0, turns)
        middle_lines(0, to_ratio)
        for piece in range(PIECES):
            end_lines(0, piece, to_ratio)
            send_ends(1, piece)
        middle_lines(1, to_blurred)
        filter_middle(ratio, 1, to_estimate, 0, early)
        for piece in range(PIECES):
            end_lines(1, piece, to_blurred)
        filter_ends(ratio, 1, to_estimate)
        if more:
            forward_ends(estimate)
        filter_middle(ratio, 1, to_estimate, early, turns)

    for chunk in range(CHUNKS):

        @pl.loop(chunk * (planes // CHUNKS), (chunk + 1) * (planes // CHUNKS), unroll=unroll)
        def _(plane):
            value = lines(estimate, plane, 0, groups).T
            for target in range(count_gy):
                stage[target, plane] = value[target * lines_x : (target + 1) * lines_x]

        for step_gy in range(count_gy):
            target = lax.rem(gy + 1 + step_gy, count_gy)

            @pl.when(is_own(target))
            def _():
                own_copy(chunk).start()

            @pl.when(jnp.logical_not(is_own(target)))
            def _():
                out_copy(chunk, target).start()

    for channel in range(channels):

        @pl.loop(0, chunks)
        def _(chunk):
            @pl.when(jnp.logical_not(is_own_plane(channel, chunk)))
            def _():
                plane_copy(channel, chunk).wait_send()

    for chunk in range(CHUNKS):
        part = pl.ds(chunk * (planes // CHUNKS), planes // CHUNKS)
        for target in range(count_gy):

            @pl.when(is_own(target))
            def _():
                own_copy(chunk).wait()

            @pl.when(jnp.logical_not(is_own(target)))
            def _():
                out_copy(chunk, target).wait_send()

        for channel in range(channels):
            for slot in range(per_gx):
                here = jnp.logical_and(channel == mine, place == core * per_gx + slot)

                @pl.when(jnp.logical_not(here))
                def _():
                    pltpu.make_async_remote_copy(
                        src_ref=stage.at[0, part],
                        dst_ref=landing(channel, slot, part),
                        send_sem=out_send.at[chunk, 0],
                        recv_sem=out_recv.at[chunk, channel, slot],
                        device_id=(gx, gy),
                        device_id_type=MESH,
                    ).wait_recv()


def hand_over(source, target, held, load_sem, store_sem):
    channels, planes = source.shape[:2]
    part = planes // MOVES
    spots = [(channel, pl.ds(move * part, part)) for channel in range(channels) for move in range(MOVES)]

    def load(index):
        spot = spots[index]
        return pltpu.make_async_copy(source.at[spot], held.at[spot], load_sem.at[index])

    def store(index):
        spot = spots[index]
        return pltpu.make_async_copy(held.at[spot], target.at[spot], store_sem.at[index])

    for index in range(len(spots)):
        load(index).start()
    for index in range(len(spots)):
        load(index).wait()
        store(index).start()
    for index in range(len(spots)):
        store(index).wait()


def local(raw_stack, psf_taps):
    channels, own_planes, lines_x, lines_y = raw_stack.shape
    half_taps = psf_taps.shape[2] // 2
    count_gx = lax.axis_size("gx")
    count_gy = lax.axis_size("gy")
    pairs = count_gx // 2
    cells = lines_y // (pairs * count_gy)
    planes = own_planes * count_gx * count_gy
    edge = -(-half_taps // SUB) * SUB

    block = min(lines_y, 256)
    groups = cells // SUB
    outer = edge // SUB
    per_gx = count_gy // 2
    block_x = lines_x // count_gy
    field = pltpu.VMEM((groups, planes, SUB, lines_x), jnp.float32)
    wide = pltpu.VMEM((groups + 2 * outer, planes, SUB, lines_x), jnp.float32)
    shape = (channels, planes, block_x, per_gx * cells)
    if cells % 128:
        shape = (channels, per_gx, planes, block_x, cells)
    gathered = pl.pallas_call(
        functools.partial(deconvolve_kernel, count_gx, count_gy, edge),
        out_shape=jax.ShapeDtypeStruct(shape, jnp.float32),
        in_specs=[pl.BlockSpec(memory_space=pl.ANY), pl.BlockSpec(memory_space=pltpu.SMEM)],
        out_specs=pl.BlockSpec(memory_space=pl.ANY),
        scratch_shapes=[
            field,
            field,
            field,
            wide,
            wide,
            pltpu.VMEM((planes, groups, SUB, lines_x), jnp.float32),
            pltpu.VMEM((count_gy, planes, block_x, cells), jnp.float32),
            pltpu.VMEM((2 * block, lines_y), jnp.bfloat16),
            pltpu.VMEM((2 * lines_x, lines_y), jnp.bfloat16),
            pltpu.VMEM((2 * lines_x, lines_x), jnp.bfloat16),
            pltpu.VMEM((2, planes, 3 * planes), jnp.bfloat16),
            pltpu.VMEM((2, 2 * lines_x, 2 * lines_x), jnp.bfloat16),
            pltpu.VMEM((2, 2 * max(cells - 2 * edge, edge), 2 * cells), jnp.bfloat16),
            pltpu.VMEM((2, 2 * edge, 6 * edge), jnp.bfloat16),
            pltpu.VMEM((lines_x, lines_y), jnp.float32),
            pltpu.SemaphoreType.DMA((2, 2, PIECES)),
            pltpu.SemaphoreType.DMA((2, 2, PIECES)),
            pltpu.SemaphoreType.DMA((CHUNKS, count_gy)),
            pltpu.SemaphoreType.DMA((CHUNKS, channels, per_gx)),
            pltpu.SemaphoreType.DMA((CHUNKS,)),
            pltpu.SemaphoreType.DMA((planes,)),
            pltpu.SemaphoreType.DMA((planes,)),
            pltpu.SemaphoreType.DMA,
        ],
        compiler_params=pltpu.CompilerParams(
            collective_id=0, has_side_effects=True, vmem_limit_bytes=67043328
        ),
    )(raw_stack, psf_taps)
    if cells % 128:
        gathered = jnp.transpose(gathered, (0, 2, 3, 1, 4))
        return gathered.reshape(channels, planes, block_x, per_gx * cells)
    return pl.pallas_call(
        hand_over,
        out_shape=jax.ShapeDtypeStruct(shape, jnp.float32),
        in_specs=[pl.BlockSpec(memory_space=pl.ANY)],
        out_specs=pl.BlockSpec(memory_space=pl.ANY),
        scratch_shapes=[
            pltpu.VMEM(shape, jnp.float32),
            pltpu.SemaphoreType.DMA((channels * MOVES,)),
            pltpu.SemaphoreType.DMA((channels * MOVES,)),
        ],
        compiler_params=pltpu.CompilerParams(vmem_limit_bytes=67043328),
    )(gathered)


def solution(mesh):
    in_specs = (P(None, ("gx", "gy"), None, None), P())
    out_specs = P(None, None, "gy", "gx")
    return jax.shard_map(local, mesh=mesh, in_specs=in_specs, out_specs=out_specs, check_vma=False)
```
